128 devices in a mesh: seq: 16 (over y, z), head: 8 (over x, core).
Axes of the slice: x: 4, y: 4, z: 4, core: 2. Of those that a mesh axis runs over, the one named last changes fastest.
Arguments:
- queries: bfloat16 [16384, 8192], P('seq', 'head'), may hold values from -6 to 6
- keys: bfloat16 [16384, 8192], P('seq', 'head'), may hold values from -6 to 6
- values: bfloat16 [16384, 8192], P('seq', 'head'), may hold values from -6 to 6
- out_grad: bfloat16 [16384, 8192], P('seq', 'head'), may hold values from -6 to 6
- level_table: float32 [5, 256], replicated, may hold values from 0.05 to 0.5
- table_index: int32 [16384], P('seq'), may hold values from 0 to 255
- reach: int32 [16], P('seq'), may hold values from 1 to 4, as said below
Outputs:
- query_grad: bfloat16 [16384, 8192], P('seq', 'head')
- key_grad: bfloat16 [16384, 8192], P('seq', 'head')
- value_grad: bfloat16 [16384, 8192], P('seq', 'head')
- table_grad: float32 [5, 256], replicated
The draws below stay inside these ranges and needn't reach their ends.
Inputs may be any that keep to these rules, and one draw needn't show every extreme that they name: Some group has reach 4 and some has reach 1.
All inputs are finite; a program needn't handle non-finite values.
Results may differ from the reference program's by a relative error of at most 0.0056.
Values sent between devices are 32-bit elements; how exact they have to be, the bound alone decides.
No kernel may reach another device: no remote copies, remote signals or barrier semaphores. Data moves between devices by JAX's collectives and lax.ppermute only.
A program may use at most 128 MiB of HBM per device.

```python
import math
import jax
import jax.numpy as jnp
from jax import lax

DH = 128
HEADS = 64
L_DEV = 1024
NTAB = 256
LEVELS = 4
TOKENS = 16384
N_SEQ = 16


def draw_reach(key, part):
    reach = jax.random.randint(key, (N_SEQ,), 1, LEVELS + 1)
    order = jax.random.permutation(jax.random.fold_in(key, 7), N_SEQ)
    reach = reach.at[order[0]].set(LEVELS)
    reach = reach.at[order[1]].set(1)
    return reach.astype(jnp.int32)


def set_ends(values, rng, low, high):
    place = [jax.random.randint(jax.random.fold_in(rng, axis), (), 0, length) for axis, length in enumerate(values.shape)]
    main_axis = values.shape.index(max(values.shape))
    neighbour = place[:main_axis] + [(place[main_axis] + 1) % values.shape[main_axis]] + place[main_axis + 1:]
    return values.at[tuple(place)].set(low).at[tuple(neighbour)].set(high)


def steps_of(stream_key, dims, pieces, smallest, top_value):
    level = 1.0
    for dim, blocks in pieces:
        draws = jax.random.uniform(jax.random.fold_in(jax.random.fold_in(stream_key, 6), dim), (blocks,), jnp.float32, smallest / len(pieces), top_value / len(pieces))
        level = level * jnp.repeat(jnp.exp(draws), dims[dim] // blocks).reshape((-1,) + (1,) * (len(dims) - 1 - dim))
    return level


def centred(stream_key, dims, spread, most, split=(), kind=jnp.bfloat16):
    gain = steps_of(stream_key, dims, split, -0.22, 0.18) if split else 1.0
    drawn = jax.random.normal(stream_key, dims, jnp.float32) * spread * gain
    return jnp.minimum(jnp.maximum(drawn, -most), most).astype(kind)


def setup_inputs(seed: int = 0) -> dict:
    key_list = jax.random.split(jax.random.key(seed), 8)
    return {
        "queries": centred(key_list[0], (TOKENS, HEADS * DH), 1.0, 6.0, ((0, 16), (1, 8))),
        "keys": centred(key_list[1], (TOKENS, HEADS * DH), 1.0, 6.0, ((0, 16), (1, 8))),
        "values": centred(key_list[2], (TOKENS, HEADS * DH), 1.0, 6.0, ((0, 16), (1, 8))),
        "out_grad": centred(key_list[3], (TOKENS, HEADS * DH), 1.0, 6.0, ((0, 16), (1, 8))),
        "level_table": jnp.clip(jnp.exp(jax.random.uniform(key_list[4], (LEVELS + 1, NTAB), jnp.float32, math.log(0.05), math.log(0.5))), 0.05, 0.5),
        "table_index": set_ends(jax.random.randint(key_list[5], (TOKENS,), 0, NTAB), jax.random.fold_in(key_list[5], 1), 0, NTAB - 1).astype(jnp.int32),
        "reach": draw_reach(jax.random.fold_in(key_list[7], 71), 0),
    }


precise = lax.Precision.HIGHEST


def rounded(array):
    return lax.optimization_barrier(array.astype(jnp.bfloat16)).astype(jnp.float32)


def level_between(target, source, levels):
    crossed = jnp.bitwise_xor(target, source)
    height = jnp.zeros_like(crossed)
    for exponent in range(levels):
        height = height + (crossed >= 2 ** exponent).astype(jnp.int32)
    return jnp.where(source < target, height, 0)


def reference(queries, keys, values, out_grad, level_table, table_index, reach):
    scale = 1.0 / DH
    count = L_DEV * N_SEQ
    weights = jnp.take(level_table, table_index, axis=1).T
    group_of = jnp.arange(count, dtype=jnp.int32) // L_DEV
    active = (jnp.arange(1, LEVELS + 1, dtype=jnp.int32)[None, :] <= reach[group_of][:, None]).astype(jnp.float32)
    near_weight = weights[:, 0].reshape(N_SEQ, L_DEV)
    far_weight = (weights[:, 1:] * active).reshape(N_SEQ, L_DEV, LEVELS)
    group_ids = jnp.arange(N_SEQ, dtype=jnp.int32)
    height = level_between(group_ids[:, None], group_ids[None, :], LEVELS)
    pick = (height[:, :, None] == jnp.arange(1, LEVELS + 1, dtype=jnp.int32)[None, None, :]).astype(jnp.float32)
    positions = jnp.arange(L_DEV, dtype=jnp.int32)
    causal = (positions[:, None] >= positions[None, :]).astype(jnp.float32)
    coef = scale * near_weight[:, :, None] * causal[None]

    def head_step(carry, head_index):
        start = head_index * DH

        def cut(array):
            return lax.dynamic_slice_in_dim(array, start, DH, 1).astype(jnp.float32).reshape(N_SEQ, L_DEV, DH)

        query_one, key_one, value_one, grad_one = cut(queries), cut(keys), cut(values), cut(out_grad)
        group_state = jnp.einsum("csd,cse->cde", key_one, value_one, precision=precise)
        level_state = jnp.einsum("csl,sde->clde", pick, group_state, precision=precise)
        state_bf = rounded(level_state)
        reads = jnp.einsum("cte,clde->ctld", grad_one, state_bf, precision=precise)
        weighted = rounded(query_one[:, :, None, :] * far_weight[:, :, :, None])
        grad_part = jnp.einsum("ctld,cte->clde", weighted, grad_one, precision=precise)
        returned = jnp.einsum("csl,clde->sde", pick, grad_part, precision=precise)
        returned_bf = rounded(returned)
        scores = jnp.einsum("ctd,csd->cts", query_one, key_one, precision=precise)
        probs = rounded(scores * coef)
        grad_probs = jnp.einsum("cte,cse->cts", grad_one, value_one, precision=precise)
        grad_scores = rounded(grad_probs * coef)
        query_grad = jnp.einsum("cts,csd->ctd", grad_scores, key_one, precision=precise)
        query_grad = query_grad + scale * jnp.sum(reads * far_weight[:, :, :, None], axis=2)
        key_grad = jnp.einsum("cts,ctd->csd", grad_scores, query_one, precision=precise)
        key_grad = key_grad + scale * jnp.einsum("cse,cde->csd", value_one, returned_bf, precision=precise)
        value_grad = jnp.einsum("cts,cte->cse", probs, grad_one, precision=precise)
        value_grad = value_grad + scale * jnp.einsum("csd,cde->cse", key_one, returned_bf, precision=precise)
        near_lambda = scale * jnp.sum(causal[None] * scores * grad_probs, axis=2)
        far_lambda = scale * jnp.sum(reads * query_one[:, :, None, :], axis=3)
        lambda_part = jnp.concatenate([near_lambda[:, :, None], far_lambda], 2).reshape(count, LEVELS + 1)
        outputs = (query_grad.reshape(count, DH).astype(jnp.bfloat16), key_grad.reshape(count, DH).astype(jnp.bfloat16), value_grad.reshape(count, DH).astype(jnp.bfloat16))
        return carry + lambda_part, outputs

    initial = jnp.zeros((count, LEVELS + 1), jnp.float32)
    total, stacked = lax.scan(head_step, initial, jnp.arange(HEADS, dtype=jnp.int32))
    query_grad, key_grad, value_grad = [jnp.transpose(piece, (1, 0, 2)).reshape(count, HEADS * DH) for piece in stacked]
    lambda_grad = total * jnp.concatenate([jnp.ones((count, 1), jnp.float32), active], 1)
    onehot = (table_index[:, None] == jnp.arange(NTAB, dtype=jnp.int32)[None, :]).astype(jnp.float32)
    table_grad = jnp.dot(lambda_grad.T, onehot, precision=precise) / count
    return query_grad, key_grad, value_grad, table_grad
```

```python
import functools

import jax
import jax.numpy as jnp
from jax import lax
from jax.experimental import pallas as pl
from jax.experimental.pallas import tpu as pltpu
from jax.sharding import PartitionSpec as P

DH = 128
CHUNK = 256

precise = lax.Precision.HIGHEST
f32 = jnp.float32
bf16 = jnp.bfloat16


def mm(a, b, ca, cb):
    return lax.dot_general(a, b, (((ca,), (cb,)), ((), ())), preferred_element_type=f32)


def states_kernel(bits, q_ref, k_ref, v_ref, g_ref, w_ref, near_ref, far_ref):
    q = q_ref[...]
    g = g_ref[...].astype(f32)
    own = mm(k_ref[...], v_ref[...], 0, 0)
    w = w_ref[...]
    parts = [(g * w[:, l : l + 1]).astype(bf16) for l in range(1, 5)]
    grads = mm(q, jnp.concatenate(parts, 1), 0, 0)
    for l in range(4):
        x = jnp.where(bits[l] > 0, grads[:, l * DH : (l + 1) * DH], own)
        if l < 2:
            near_ref[l, 0] = x
        else:
            far_ref[0, l - 2, 0] = x


def group_kernel(q_ref, k_ref, v_ref, g_ref, w_ref, qn_ref, kn_ref, vn_ref, lam_ref):
    head = pl.program_id(0)
    scale = 1.0 / DH
    length = q_ref.shape[0]
    count = length // CHUNK
    rows = lax.broadcasted_iota(jnp.int32, (CHUNK, CHUNK), 0)
    cols = lax.broadcasted_iota(jnp.int32, (CHUNK, CHUNK), 1)
    causal = rows >= cols

    @pl.when(head == 0)
    def _():
        lam_ref[...] = jnp.zeros_like(lam_ref)

    state = jnp.zeros((DH, DH), f32)
    gps, scs, qss = [], [], []
    for i in range(count):
        at = pl.ds(i * CHUNK, CHUNK)
        q, k, v, g = q_ref[at, :], k_ref[at, :], v_ref[at, :], g_ref[at, :]
        w0 = w_ref[at, 0:1]
        qf = q.astype(f32)
        qs = (qf * w0).astype(bf16)
        gp = jnp.where(causal, mm(g, v, 1, 1), 0.0).astype(bf16)
        sc = jnp.where(causal, mm(qs, k, 1, 1), 0.0).astype(bf16)
        u = mm(gp, k, 1, 0)
        if i > 0:
            u = u + mm(g, state.astype(bf16), 1, 1)
        lam_ref[at, :] += qf * u
        qn_ref[at, :] = (scale * w0) * u
        if i < count - 1:
            state = state + mm(k, v, 0, 0)
        gps.append(gp)
        scs.append(sc)
        qss.append(qs)
    state = jnp.zeros((DH, DH), f32)
    for i in reversed(range(count)):
        at = pl.ds(i * CHUNK, CHUNK)
        k, v, g = k_ref[at, :], v_ref[at, :], g_ref[at, :]
        kn = mm(gps[i], qss[i], 0, 0)
        vn = mm(scs[i], g, 0, 0)
        if i < count - 1:
            sb = state.astype(bf16)
            kn = kn + mm(v, sb, 1, 1)
            vn = vn + mm(k, sb, 1, 0)
        kn_ref[at, :] = scale * kn
        vn_ref[at, :] = scale * vn
        if i > 0:
            state = state + mm(qss[i], g, 0, 0)


def reads_kernel(bits, q_ref, g_ref, w_ref, qn_ref, lam0_ref, y1_ref, y2_ref, y3_ref, out_ref, lam_ref, acc):
    head = pl.program_id(0)
    scale = 1.0 / DH

    @pl.when(head == 0)
    def _():
        acc[...] = jnp.zeros_like(acc)

    ys = [y1_ref[0], y2_ref[0], y3_ref[0, 0, 0], y3_ref[0, 1, 0]]
    states = [jnp.where(bits[l] > 0, ys[l], 0.0).astype(bf16) for l in range(4)]
    reads = mm(g_ref[...], jnp.concatenate(states, 0), 1, 1)
    q = q_ref[...].astype(f32)
    w = w_ref[...]
    total = None
    for l in range(4):
        read = reads[:, l * DH : (l + 1) * DH]
        acc[l] += q * read
        term = w[:, l + 1 : l + 2] * read
        total = term if total is None else total + term
    out_ref[...] = (qn_ref[...] + scale * total).astype(bf16)

    @pl.when(head == pl.num_programs(0) - 1)
    def _():
        lane = lax.broadcasted_iota(jnp.int32, (1, DH), 1)
        lam = jnp.where(lane == 0, jnp.sum(lam0_ref[...], 1, keepdims=True), 0.0)
        for l in range(4):
            here = (lane == l + 1) & (bits[4] > l)
            lam = jnp.where(here, jnp.sum(acc[l], 1, keepdims=True), lam)
        lam_ref[...] = scale * lam


def returns_kernel(bits, k_ref, v_ref, kn_ref, vn_ref, y1_ref, y2_ref, y3_ref, key_ref, value_ref):
    scale = 1.0 / DH
    ys = [y1_ref[0], y2_ref[0], y3_ref[0, 0, 0], y3_ref[0, 1, 0]]
    total = None
    for l in range(4):
        y = jnp.where(bits[l] > 0, 0.0, ys[l])
        total = y if total is None else total + y
    ret = total.astype(bf16)
    key_ref[...] = (kn_ref[...] + scale * mm(v_ref[...], ret, 1, 1)).astype(bf16)
    value_ref[...] = (vn_ref[...] + scale * mm(k_ref[...], ret, 1, 0)).astype(bf16)


def flip(x, axis, mask):
    return lax.ppermute(x, axis, [(i, i ^ mask) for i in range(lax.axis_size(axis))])


def local(queries, keys, values, out_grad, level_table, table_index, reach):
    length = queries.shape[0]
    heads = queries.shape[1] // DH
    span = lax.axis_size("seq")
    group = lax.axis_index("seq")
    bits = jnp.bitwise_and(jnp.right_shift(group, jnp.arange(4, dtype=jnp.int32)), 1)
    bits = jnp.concatenate([bits, reach.astype(jnp.int32)])
    picker = (
        table_index[:, None] == jnp.arange(level_table.shape[1], dtype=jnp.int32)[None, :]
    ).astype(f32)
    level_ids = jnp.arange(8, dtype=jnp.int32)
    table = jnp.pad(level_table, ((0, 3), (0, 0)))
    table = jnp.where((level_ids <= reach[0])[:, None], table, 0.0)
    weights = jnp.dot(picker, table.T, precision=precise)

    token_spec = pl.BlockSpec((length, DH), lambda h, *_: (0, h))
    fixed = lambda shape: pl.BlockSpec(shape, lambda h, *_: (0,) * len(shape))
    w_spec = fixed((length, 8))
    near_spec = pl.BlockSpec((2, 1, DH, DH), lambda h, *_: (0, h, 0, 0))
    state_spec = pl.BlockSpec((1, DH, DH), lambda h, *_: (h, 0, 0))
    far_spec = pl.BlockSpec((1, 2, 1, DH, DH), lambda h, *_: (h // 2, 0, h % 2, 0, 0))
    params = pltpu.CompilerParams(dimension_semantics=("arbitrary",), vmem_limit_bytes=40 * 2**20)

    near, far = pl.pallas_call(
        states_kernel,
        grid_spec=pltpu.PrefetchScalarGridSpec(
            num_scalar_prefetch=1,
            grid=(heads,),
            in_specs=[token_spec] * 4 + [w_spec],
            out_specs=[near_spec, far_spec],
        ),
        out_shape=[
            jax.ShapeDtypeStruct((2, heads, DH, DH), f32),
            jax.ShapeDtypeStruct((4, 2, heads // 4, DH, DH), f32),
        ],
        compiler_params=params,
        name="states",
    )(bits, queries, keys, values, out_grad, weights)

    rings = [[4 * y + z for z in range(4)] for y in range(span // 4)]
    got = lax.all_to_all(far, "seq", 0, 0, axis_index_groups=rings)
    pair2 = flip(near[1], "seq", 1)
    y1 = flip(near[0], "seq", 1)
    y2 = flip(near[1] + pair2, "seq", 3)
    rows = jnp.sum(got, axis=0)
    other = flip(rows, "seq", 4)
    y3s = other[0]
    y4s = flip(rows[1] + other[1], "seq", 12)
    back = jnp.stack([y3s, y4s], 0)
    y34 = lax.all_to_all(
        jnp.broadcast_to(back[None], (4,) + back.shape), "seq", 0, 0, axis_index_groups=rings
    )

    tokens_f32 = jax.ShapeDtypeStruct((length, heads * DH), f32)
    tokens_bf16 = jax.ShapeDtypeStruct((length, heads * DH), bf16)
    qn, kn, vn, lam0 = pl.pallas_call(
        group_kernel,
        grid=(heads,),
        in_specs=[token_spec] * 4 + [w_spec],
        out_specs=[token_spec] * 3 + [fixed((length, DH))],
        out_shape=[tokens_f32] * 3 + [jax.ShapeDtypeStruct((length, DH), f32)],
        compiler_params=params,
        cost_estimate=pl.CostEstimate(flops=4 * 10**9, bytes_accessed=20 * 2**20, transcendentals=0),
        name="group",
    )(queries, keys, values, out_grad, weights)

    query_grad, lam = pl.pallas_call(
        reads_kernel,
        grid_spec=pltpu.PrefetchScalarGridSpec(
            num_scalar_prefetch=1,
            grid=(heads,),
            in_specs=[token_spec] * 2
            + [w_spec, token_spec, fixed((length, DH)), state_spec, state_spec, far_spec],
            out_specs=[token_spec, fixed((length, DH))],
            scratch_shapes=[pltpu.VMEM((4, length, DH), f32)],
        ),
        out_shape=[tokens_bf16, jax.ShapeDtypeStruct((length, DH), f32)],
        compiler_params=params,
        cost_estimate=pl.CostEstimate(flops=2 * 10**9, bytes_accessed=10 * 2**20, transcendentals=0),
        name="reads",
    )(bits, queries, out_grad, weights, qn, lam0, y1, y2, y34)

    total = lax.dot_general(lam[:, :8], picker, (((0,), (0,)), ((), ())), precision=precise)
    for mask in (1, 2, 6):
        total = total + flip(total, "head", mask)
    for mask in (1, 3, 4, 12):
        total = total + flip(total, "seq", mask)
    table_grad = total[: level_table.shape[0]] / (length * span)

    key_grad, value_grad = pl.pallas_call(
        returns_kernel,
        grid_spec=pltpu.PrefetchScalarGridSpec(
            num_scalar_prefetch=1,
            grid=(heads,),
            in_specs=[token_spec] * 4 + [state_spec, state_spec, far_spec],
            out_specs=[token_spec] * 2,
        ),
        out_shape=[tokens_bf16] * 2,
        compiler_params=params,
        cost_estimate=pl.CostEstimate(flops=10**9, bytes_accessed=16 * 2**20, transcendentals=0),
        name="returns",
    )(bits, keys, values, kn, vn, y1, y2, y34)
    return query_grad, key_grad, value_grad, table_grad


def solution(mesh):
    return jax.shard_map(
        local,
        mesh=mesh,
        in_specs=(
            P("seq", "head"),
            P("seq", "head"),
            P("seq", "head"),
            P("seq", "head"),
            P(),
            P("seq"),
            P("seq"),
        ),
        out_specs=(P("seq", "head"), P("seq", "head"), P("seq", "head"), P()),
        check_vma=False,
    )
```

```python
import functools

import jax
import jax.numpy as jnp
from jax import lax
from jax.experimental import pallas as pl
from jax.experimental.pallas import tpu as pltpu
from jax.sharding import PartitionSpec as P

DH = 128
CHUNK = 256

precise = lax.Precision.HIGHEST
f32 = jnp.float32
bf16 = jnp.bfloat16


def mm(a, b, ca, cb):
    return lax.dot_general(a, b, (((ca,), (cb,)), ((), ())), preferred_element_type=f32)


def states_kernel(bits, q_hbm, k_hbm, v_hbm, g_hbm, w_ref, near1_ref, near2_ref, *rest):
    far_refs, buf, sem = rest[:4], rest[4], rest[5]
    sources = (q_hbm, k_hbm, v_hbm, g_hbm)
    wide = buf.shape[-1]
    each = wide // DH

    def copy(j, a):
        cols = pl.ds(pl.multiple_of((bits[5] ^ j) * wide, wide), wide)
        return pltpu.make_async_copy(sources[a].at[:, cols], buf.at[j, a], sem.at[j, a])

    for j in range(4):
        for a in range(4):
            copy(j, a).start()
    w = w_ref[...]
    for j in range(4):
        for a in range(4):
            copy(j, a).wait()
        for i in range(each):
            c = slice(i * DH, (i + 1) * DH)
            head = (bits[5] ^ j) * each + i
            own = mm(buf[j, 2, :, c].T, buf[j, 1, :, c], 1, 0)
            gt = buf[j, 3, :, c].T.astype(f32)
            parts = [(gt * w[l : l + 1, :]).astype(bf16) for l in range(1, 5)]
            grads = mm(jnp.concatenate(parts, 0), buf[j, 0, :, c], 1, 0)
            xs = [
                jnp.where(bits[l] > 0, grads[l * DH : (l + 1) * DH], own) for l in range(4)
            ]
            near1_ref[head] = xs[0]
            near2_ref[head] = xs[1]
            far_refs[j][0, i] = xs[2]
            far_refs[j][1, i] = xs[3]


def group_kernel(q_ref, k_ref, v_ref, g_ref, w_ref, qn_ref, kn_ref, vn_ref, lam_ref):
    head = pl.program_id(0)
    scale = 1.0 / DH
    length = q_ref.shape[0]
    count = length // CHUNK
    rows = lax.broadcasted_iota(jnp.int32, (CHUNK, CHUNK), 0)
    cols = lax.broadcasted_iota(jnp.int32, (CHUNK, CHUNK), 1)
    causal = rows >= cols

    @pl.when(head == 0)
    def _():
        lam_ref[...] = jnp.zeros_like(lam_ref)

    state = jnp.zeros((DH, DH), f32)
    gps, scs, qss = [], [], []
    for i in range(count):
        at = pl.ds(i * CHUNK, CHUNK)
        q, k, v, g = q_ref[at, :], k_ref[at, :], v_ref[at, :], g_ref[at, :]
        w0 = w_ref[at, 0:1]
        qf = q.astype(f32)
        qs = (qf * w0).astype(bf16)
        gp = jnp.where(causal, mm(g, v, 1, 1), 0.0).astype(bf16)
        sc = jnp.where(causal, mm(qs, k, 1, 1), 0.0).astype(bf16)
        u = mm(gp, k, 1, 0)
        if i > 0:
            u = u + mm(g, state.astype(bf16), 1, 1)
        lam_ref[at, :] += qf * u
        qn_ref[at, :] = (scale * w0) * u
        if i < count - 1:
            state = state + mm(k, v, 0, 0)
        gps.append(gp)
        scs.append(sc)
        qss.append(qs)
    state = jnp.zeros((DH, DH), f32)
    for i in reversed(range(count)):
        at = pl.ds(i * CHUNK, CHUNK)
        k, v, g = k_ref[at, :], v_ref[at, :], g_ref[at, :]
        kn = mm(gps[i], qss[i], 0, 0)
        vn = mm(scs[i], g, 0, 0)
        if i < count - 1:
            sb = state.astype(bf16)
            kn = kn + mm(v, sb, 1, 1)
            vn = vn + mm(k, sb, 1, 0)
        kn_ref[at, :] = scale * kn
        vn_ref[at, :] = scale * vn
        if i > 0:
            state = state + mm(qss[i], g, 0, 0)


def gather_states(bits, keep, st, y1_ref, y2a_ref, y2b_ref, y3_refs, y4_refs, put):
    heads = y1_ref.shape[0]
    each = heads // 4
    for j in range(4):
        for i in range(each):
            head = (bits[5] ^ j) * each + i
            ys = (
                y1_ref[head],
                y2a_ref[head] + y2b_ref[head],
                y3_refs[j][i],
                y4_refs[j][i],
            )
            put(st, head, [jnp.where(bits[l] == keep, ys[l], 0.0) for l in range(4)])


def reads_kernel(bits, q_ref, g_ref, w_ref, qn_ref, lam0_ref, y1_ref, y2a_ref, y2b_ref, *rest):
    y3_refs, y4_refs, (out_ref, lam_ref, st) = rest[:4], rest[4:8], rest[8:]
    scale = 1.0 / DH
    heads = y1_ref.shape[0]

    def put(st, head, parts):
        st[head] = jnp.concatenate(parts, 1).astype(bf16)

    @pl.when(pl.program_id(0) == 0)
    def _():
        gather_states(bits, 1, st, y1_ref, y2a_ref, y2b_ref, y3_refs, y4_refs, put)

    tile = q_ref.shape[0]
    w = w_ref[...]
    wide = [jnp.broadcast_to(w[:, l : l + 1], (tile, DH)) for l in range(1, 5)]
    acc = [None] * 4
    for h in range(heads):
        c = slice(h * DH, (h + 1) * DH)
        reads = mm(g_ref[:, c], st[h], 1, 0)
        q = q_ref[:, c].astype(f32)
        total = None
        for l in range(4):
            read = reads[:, l * DH : (l + 1) * DH]
            product = q * read
            acc[l] = product if acc[l] is None else acc[l] + product
            term = wide[l] * read
            total = term if total is None else total + term
        out_ref[:, c] = (qn_ref[:, c] + scale * total).astype(bf16)
    lane = lax.broadcasted_iota(jnp.int32, (1, DH), 1)
    lam = jnp.where(lane == 0, jnp.sum(lam0_ref[...], 1, keepdims=True), 0.0)
    for l in range(4):
        here = (lane == l + 1) & (bits[4] > l)
        lam = jnp.where(here, jnp.sum(acc[l], 1, keepdims=True), lam)
    lam_ref[...] = scale * lam


def returns_kernel(bits, k_ref, v_ref, kn_ref, vn_ref, y1_ref, y2a_ref, y2b_ref, *rest):
    y3_refs, y4_refs, (key_ref, value_ref, st) = rest[:4], rest[4:8], rest[8:]
    scale = 1.0 / DH
    heads = y1_ref.shape[0]

    def put(st, head, parts):
        st[head] = (parts[0] + parts[1] + parts[2] + parts[3]).astype(bf16)

    @pl.when(pl.program_id(0) == 0)
    def _():
        gather_states(bits, 0, st, y1_ref, y2a_ref, y2b_ref, y3_refs, y4_refs, put)

    for h in range(heads):
        c = slice(h * DH, (h + 1) * DH)
        key_ref[:, c] = (kn_ref[:, c] + scale * mm(v_ref[:, c], st[h], 1, 0)).astype(bf16)
        value_ref[:, c] = (vn_ref[:, c] + scale * mm(k_ref[:, c], st[h], 1, 1)).astype(bf16)


def flip(x, axis, mask):
    return lax.ppermute(x, axis, [(i, i ^ mask) for i in range(lax.axis_size(axis))])


def local(queries, keys, values, out_grad, level_table, table_index, reach):
    length = queries.shape[0]
    heads = queries.shape[1] // DH
    span = lax.axis_size("seq")
    group = lax.axis_index("seq")
    bits = jnp.bitwise_and(jnp.right_shift(group, jnp.arange(4, dtype=jnp.int32)), 1)
    place = jnp.bitwise_and(group, 3)
    bits = jnp.concatenate([bits, reach.astype(jnp.int32), place[None].astype(jnp.int32)])
    picker = (
        table_index[:, None] == jnp.arange(level_table.shape[1], dtype=jnp.int32)[None, :]
    ).astype(f32)
    level_ids = jnp.arange(8, dtype=jnp.int32)
    table = jnp.pad(level_table, ((0, 3), (0, 0)))
    table = jnp.where((level_ids <= reach[0])[:, None], table, 0.0)
    weights = jnp.dot(picker, table.T, precision=precise)
    each = heads // 4

    whole = pl.BlockSpec(memory_space=pltpu.VMEM)
    near, near2, *far = pl.pallas_call(
        states_kernel,
        in_specs=[pl.BlockSpec(memory_space=pltpu.SMEM)]
        + [pl.BlockSpec(memory_space=pl.ANY)] * 4
        + [whole],
        out_specs=[whole] * 6,
        out_shape=[jax.ShapeDtypeStruct((heads, DH, DH), f32)] * 2
        + [jax.ShapeDtypeStruct((2, each, DH, DH), f32)] * 4,
        scratch_shapes=[
            pltpu.VMEM((4, 4, length, each * DH), bf16),
            pltpu.SemaphoreType.DMA((4, 4)),
        ],
        compiler_params=pltpu.CompilerParams(vmem_limit_bytes=60 * 2**20),
        name="states",
    )(bits, queries, keys, values, out_grad, weights.T)

    rows = (far[0] + flip(far[2], "seq", 2)) + (flip(far[1], "seq", 1) + flip(far[3], "seq", 3))
    rows, near, near2 = lax.optimization_barrier((rows, near, near2))
    other = flip(rows, "seq", 4)
    y1 = flip(near, "seq", 1)
    y2a = flip(near2, "seq", 3)
    y2b = flip(near2, "seq", 2)
    y3 = other[0]
    y4 = flip(rows[1] + other[1], "seq", 12)
    y3s = [y3] + [flip(y3, "seq", m) for m in (1, 2, 3)]
    y4s = [y4] + [flip(y4, "seq", m) for m in (1, 2, 3)]
    arrived = (y1, y2a, y2b, *y3s, *y4s)

    token_spec = pl.BlockSpec((length, DH), lambda h, *_: (0, h))
    fixed = lambda shape: pl.BlockSpec(shape, lambda h, *_: (0,) * len(shape))
    tile = 256
    tile_spec = pl.BlockSpec((tile, heads * DH), lambda i, *_: (i, 0))
    lam_spec = pl.BlockSpec((tile, DH), lambda i, *_: (i, 0))
    arrived_specs = [fixed(y.shape) for y in arrived]
    params = pltpu.CompilerParams(
        dimension_semantics=("arbitrary",), vmem_limit_bytes=60 * 2**20
    )
    tokens_f32 = jax.ShapeDtypeStruct((length, heads * DH), f32)
    tokens_bf16 = jax.ShapeDtypeStruct((length, heads * DH), bf16)
    qn, kn, vn, lam0 = pl.pallas_call(
        group_kernel,
        grid=(heads,),
        in_specs=[token_spec] * 4 + [fixed((length, 8))],
        out_specs=[token_spec] * 3 + [fixed((length, DH))],
        out_shape=[tokens_f32] * 3 + [jax.ShapeDtypeStruct((length, DH), f32)],
        compiler_params=params,
        cost_estimate=pl.CostEstimate(flops=4 * 10**9, bytes_accessed=20 * 2**20, transcendentals=0),
        name="group",
    )(queries, keys, values, out_grad, weights)

    query_grad, lam = pl.pallas_call(
        reads_kernel,
        grid_spec=pltpu.PrefetchScalarGridSpec(
            num_scalar_prefetch=1,
            grid=(length // tile,),
            in_specs=[tile_spec] * 2
            + [pl.BlockSpec((tile, 8), lambda i, *_: (i, 0)), tile_spec, lam_spec]
            + arrived_specs,
            out_specs=[tile_spec, lam_spec],
            scratch_shapes=[pltpu.VMEM((heads, DH, 4 * DH), bf16)],
        ),
        out_shape=[tokens_bf16, jax.ShapeDtypeStruct((length, DH), f32)],
        compiler_params=params,
        cost_estimate=pl.CostEstimate(flops=2 * 10**9, bytes_accessed=10 * 2**20, transcendentals=0),
        name="reads",
    )(bits, queries, out_grad, weights, qn, lam0, *arrived)

    total = lax.dot_general(lam[:, :8], picker, (((0,), (0,)), ((), ())), precision=precise)
    total = total + flip(total, "head", 1)
    for axis, unit in (("head", 2), ("seq", 1), ("seq", 4)):
        one, two, three = [flip(total, axis, m * unit) for m in (1, 2, 3)]
        total = (total + two) + (one + three)
    table_grad = total[: level_table.shape[0]] / (length * span)

    key_grad, value_grad = pl.pallas_call(
        returns_kernel,
        grid_spec=pltpu.PrefetchScalarGridSpec(
            num_scalar_prefetch=1,
            grid=(length // tile,),
            in_specs=[tile_spec] * 4 + arrived_specs,
            out_specs=[tile_spec] * 2,
            scratch_shapes=[pltpu.VMEM((heads, DH, DH), bf16)],
        ),
        out_shape=[tokens_bf16] * 2,
        compiler_params=params,
        cost_estimate=pl.CostEstimate(flops=10**9, bytes_accessed=16 * 2**20, transcendentals=0),
        name="returns",
    )(bits, keys, values, kn, vn, *arrived)
    return query_grad, key_grad, value_grad, table_grad


def solution(mesh):
    return jax.shard_map(
        local,
        mesh=mesh,
        in_specs=(
            P("seq", "head"),
            P("seq", "head"),
            P("seq", "head"),
            P("seq", "head"),
            P(),
            P("seq"),
            P("seq"),
        ),
        out_specs=(P("seq", "head"), P("seq", "head"), P("seq", "head"), P()),
        check_vma=False,
    )
```

```python
import jax
import jax.numpy as jnp
from jax import lax
from jax.experimental import pallas as pl
from jax.experimental.pallas import tpu as pltpu
from jax.sharding import PartitionSpec as P

DH = 128
CHUNK = 256
SCALE = 1.0 / DH
MIB = 2**20

f32 = jnp.float32
bf16 = jnp.bfloat16


def mm(a, b, ca, cb):
    return lax.dot_general(a, b, (((ca,), (cb,)), ((), ())), preferred_element_type=f32)


def place():
    group = lax.axis_index("seq")
    bits = [jnp.bitwise_and(jnp.right_shift(group, l), 1) for l in range(4)]
    return bits, jnp.bitwise_and(group, 3)


def thirds(x):
    one = x.astype(bf16)
    rest = x - one.astype(f32)
    two = rest.astype(bf16)
    return one, two, (rest - two.astype(f32)).astype(bf16)


def one_hot(index_row, size):
    ids = lax.broadcasted_iota(jnp.int32, (size, index_row.shape[1]), 0)
    return jnp.where(ids == index_row, 1.0, 0.0).astype(bf16)


def states_kernel(reach, index_ref, table_ref, q_hbm, k_hbm, v_hbm, g_hbm, w_ref, near1_ref, near2_ref, *rest):
    far_refs, buf, table, sem = rest[:4], rest[4], rest[5], rest[6]
    sources = (q_hbm, k_hbm, v_hbm, g_hbm)
    wide = buf.shape[-1]
    each = wide // DH
    bits, spot = place()

    def copy(j, a):
        cols = pl.ds(pl.multiple_of((spot ^ j) * wide, wide), wide)
        return pltpu.make_async_copy(sources[a].at[:, cols], buf.at[j, a], sem.at[j, a])

    for j in range(4):
        for a in range(4):
            copy(j, a).start()
    table[...] = jnp.zeros_like(table)
    table[0 : table_ref.shape[0], :] = table_ref[...]
    level = lax.broadcasted_iota(jnp.int32, table.shape, 0)
    picked = one_hot(index_ref[...], table.shape[1])
    pieces = thirds(jnp.where(level <= reach[0], table[...], 0.0))
    w = mm(pieces[0], picked, 1, 0) + mm(pieces[1], picked, 1, 0) + mm(pieces[2], picked, 1, 0)
    w_ref[...] = w
    for j in range(4):
        for a in range(4):
            copy(j, a).wait()
        for i in range(each):
            c = slice(i * DH, (i + 1) * DH)
            head = (spot ^ j) * each + i
            own = mm(buf[j, 2, :, c].T, buf[j, 1, :, c], 1, 0)
            gt = buf[j, 3, :, c].T.astype(f32)
            parts = [(gt * w[l : l + 1, :]).astype(bf16) for l in range(1, 5)]
            grads = mm(jnp.concatenate(parts, 0), buf[j, 0, :, c], 1, 0)
            xs = [jnp.where(bits[l] > 0, grads[l * DH : (l + 1) * DH], own) for l in range(4)]
            near1_ref[head] = xs[0]
            near2_ref[head] = xs[1]
            far_refs[j][0, i] = xs[2]
            far_refs[j][1, i] = xs[3]


def causal_mask(flip_sides):
    rows = lax.broadcasted_iota(jnp.int32, (CHUNK, CHUNK), 0)
    cols = lax.broadcasted_iota(jnp.int32, (CHUNK, CHUNK), 1)
    return rows <= cols if flip_sides else rows >= cols


def query_kernel(order, q_ref, k_ref, v_ref, g_ref, w_ref, out_ref, lam_ref):
    @pl.when(pl.program_id(0) == 0)
    def _():
        lam_ref[...] = jnp.zeros_like(lam_ref)

    causal = causal_mask(False)
    state = jnp.zeros((DH, DH), f32)
    count = q_ref.shape[0] // CHUNK
    for i in range(count):
        at = pl.ds(i * CHUNK, CHUNK)
        k, v, g = k_ref[at, :], v_ref[at, :], g_ref[at, :]
        near = jnp.where(causal, mm(g, v, 1, 1), 0.0).astype(bf16)
        u = mm(near, k, 1, 0)
        if i > 0:
            u = u + mm(g, state.astype(bf16), 1, 0)
        lam_ref[at, :] += q_ref[at, :].astype(f32) * u
        out_ref[at, :] = (SCALE * w_ref[at, 0:1]) * u
        if i < count - 1:
            state = state + mm(v, k, 0, 0)


def key_value_kernel(order, q_ref, k_ref, v_ref, g_ref, w_ref, key_ref, value_ref):
    causal = causal_mask(True)
    state = jnp.zeros((DH, DH), f32)
    count = q_ref.shape[0] // CHUNK
    for i in reversed(range(count)):
        at = pl.ds(i * CHUNK, CHUNK)
        k, v, g = k_ref[at, :], v_ref[at, :], g_ref[at, :]
        q = (q_ref[at, :].astype(f32) * w_ref[at, 0:1]).astype(bf16)
        near_key = jnp.where(causal, mm(v, g, 1, 1), 0.0).astype(bf16)
        near_value = jnp.where(causal, mm(k, q, 1, 1), 0.0).astype(bf16)
        key = mm(near_key, q, 1, 0)
        value = mm(near_value, g, 1, 0)
        if i < count - 1:
            held = state.astype(bf16)
            key = key + mm(v, held, 1, 0)
            value = value + mm(k, held, 1, 1)
        key_ref[at, :] = SCALE * key
        value_ref[at, :] = SCALE * value
        if i > 0:
            state = state + mm(g, q, 0, 0)


def level_states(keep, y1_ref, y2a_ref, y2b_ref, y3_refs, y4_refs, bits, head, j, i):
    ys = (y1_ref[head], y2a_ref[head] + y2b_ref[head], y3_refs[j][i], y4_refs[j][i])
    return [jnp.where(bits[l] == keep, ys[l], 0.0) for l in range(4)]


def reads_kernel(reach, q_ref, g_ref, w_ref, qn_ref, lam0_ref, index_ref, y1_ref, y2a_ref, y2b_ref, *rest):
    y3_refs, y4_refs, (out_hbm, table_ref, st, out_buf, sem) = rest[:4], rest[4:8], rest[8:]
    length = q_ref.shape[0]
    heads = y1_ref.shape[0]
    each = heads // 4
    tile = CHUNK
    bits, spot = place()
    for j in range(4):
        for i in range(each):
            head = (spot ^ j) * each + i
            parts = level_states(1, y1_ref, y2a_ref, y2b_ref, y3_refs, y4_refs, bits, head, j, i)
            st[head] = jnp.concatenate(parts, 1).astype(bf16)
    lane = lax.broadcasted_iota(jnp.int32, (1, DH), 1)
    table = None
    copies = []
    for t in range(length // tile):
        at = pl.ds(t * tile, tile)
        w = w_ref[at, :]
        wide = [jnp.broadcast_to(w[:, l : l + 1], (tile, DH)) for l in range(1, 5)]
        acc = [None] * 4
        for h in range(heads):
            c = slice(h * DH, (h + 1) * DH)
            reads = mm(g_ref[at, c], st[h], 1, 0)
            q = q_ref[at, c].astype(f32)
            total = None
            for l in range(4):
                read = reads[:, l * DH : (l + 1) * DH]
                product = q * read
                acc[l] = product if acc[l] is None else acc[l] + product
                term = wide[l] * read
                total = term if total is None else total + term
            out_buf[at, c] = (qn_ref[at, c] + SCALE * total).astype(bf16)
        copies.append(pltpu.make_async_copy(out_buf.at[at, :], out_hbm.at[at, :], sem.at[t]))
        copies[-1].start()
        lam = jnp.where(lane == 0, jnp.sum(lam0_ref[at, :], 1, keepdims=True), 0.0)
        for l in range(4):
            here = (lane == l + 1) & (reach[0] > l)
            lam = jnp.where(here, jnp.sum(acc[l], 1, keepdims=True), lam)
        lam = (SCALE * lam).T[:8]
        picked = one_hot(index_ref[:, at], table_ref.shape[1])
        for piece in thirds(lam):
            part = mm(piece, picked, 1, 1)
            table = part if table is None else table + part
    table_ref[...] = table
    for copy in copies:
        copy.wait()


def returns_kernel(start, order, k_ref, v_ref, kn_ref, vn_ref, y1_ref, y2a_ref, y2b_ref, *rest):
    y3_refs, y4_refs, rest = rest[:4], rest[4:8], rest[8:]
    key_hbm, value_hbm, key_buf, value_buf, st, sem = rest[-6:]
    heads = y1_ref.shape[0]
    each = heads // 4
    count = key_buf.shape[1] // DH
    near_start = start % (kn_ref.shape[1] // DH)
    bits, spot = place()
    for j in range(4):
        for i in range(each):
            head = (spot ^ j) * each + i

            @pl.when((head >= start) & (head < start + count))
            def _():
                parts = level_states(0, y1_ref, y2a_ref, y2b_ref, y3_refs, y4_refs, bits, head, j, i)
                st[head] = (parts[0] + parts[1] + parts[2] + parts[3]).astype(bf16)

    for i in range(count):
        head = start + i
        c = slice(head * DH, (head + 1) * DH)
        n = slice((near_start + i) * DH, (near_start + i + 1) * DH)
        o = slice(i * DH, (i + 1) * DH)
        key_buf[:, o] = (kn_ref[:, n] + SCALE * mm(v_ref[:, c], st[head], 1, 0)).astype(bf16)
        value_buf[:, o] = (vn_ref[:, n] + SCALE * mm(k_ref[:, c], st[head], 1, 1)).astype(bf16)
    cols = pl.ds(start * DH, count * DH)
    key_copy = pltpu.make_async_copy(key_buf, key_hbm.at[:, cols], sem.at[0])
    value_copy = pltpu.make_async_copy(value_buf, value_hbm.at[:, cols], sem.at[1])
    key_copy.start()
    value_copy.start()
    key_copy.wait()
    value_copy.wait()


def flip(x, axis, mask):
    return lax.ppermute(x, axis, [(i, i ^ mask) for i in range(lax.axis_size(axis))])


def tie(x, *deps):
    return lax.optimization_barrier((x, *deps))[0]


def local(queries, keys, values, out_grad, level_table, table_index, reach):
    length = queries.shape[0]
    heads = queries.shape[1] // DH
    each = heads // 4
    span = lax.axis_size("seq")
    names = level_table.shape[1]
    index_row = table_index.reshape(1, length)
    sds = jax.ShapeDtypeStruct
    whole = pl.BlockSpec(memory_space=pltpu.VMEM)
    scalar = pl.BlockSpec(memory_space=pltpu.SMEM)
    anywhere = pl.BlockSpec(memory_space=pl.ANY)
    limit = lambda mib: pltpu.CompilerParams(vmem_limit_bytes=mib * MIB)
    cost = lambda us: pl.CostEstimate(flops=int(us * 10**9), bytes_accessed=MIB, transcendentals=0)

    w_rows, near, near2, *far = pl.pallas_call(
        states_kernel,
        in_specs=[scalar, whole, whole] + [anywhere] * 4,
        out_specs=[whole] * 7,
        out_shape=[sds((8, length), f32)]
        + [sds((heads, DH, DH), f32)] * 2
        + [sds((2, each, DH, DH), f32)] * 4,
        scratch_shapes=[
            pltpu.VMEM((4, 4, length, each * DH), bf16),
            pltpu.VMEM((8, names), f32),
            pltpu.SemaphoreType.DMA((4, 4)),
        ],
        compiler_params=limit(60),
        name="states",
    )(reach, index_row, level_table, queries, keys, values, out_grad)
    w_cols = w_rows.T

    token_spec = lambda start: pl.BlockSpec((length, DH), lambda h: (0, h + start))
    fixed = lambda shape: pl.BlockSpec(shape, lambda h: (0,) * len(shape))

    def near_part(kernel, order, start, count, out_shape, out_specs, name):
        return pl.pallas_call(
            kernel,
            grid=(count,),
            in_specs=[scalar] + [token_spec(start)] * 4 + [fixed((length, 8))],
            out_specs=out_specs,
            out_shape=out_shape,
            compiler_params=pltpu.CompilerParams(
                dimension_semantics=("arbitrary",), vmem_limit_bytes=20 * MIB
            ),
            cost_estimate=cost(5),
            name=name,
        )(order, queries, keys, values, out_grad, w_cols)

    def key_value_part(order, start, count, name):
        shape = sds((length, count * DH), f32)
        return near_part(
            key_value_kernel, order, start, count, [shape] * 2, [token_spec(0)] * 2, name
        )

    got = [flip(far[m], "seq", m) for m in (1, 3, 2)]
    qn, lam0 = near_part(
        query_kernel,
        tie(reach, *far),
        0,
        heads,
        [sds((length, heads * DH), f32), sds((length, DH), f32)],
        [token_spec(0), fixed((length, DH))],
        "query",
    )
    got = lax.optimization_barrier((*got, qn))[:3]
    rows = (far[0] + got[2]) + (got[0] + got[1])
    other = flip(rows, "seq", 4)
    near, near2 = lax.optimization_barrier((near, near2, rows))[:2]
    y1 = flip(near, "seq", 1)
    y2a = flip(near2, "seq", 3)
    y2b = flip(near2, "seq", 2)
    half = heads // 2
    kn_a, vn_a = key_value_part(tie(reach, rows), 0, half, "key_value_a")
    other = tie(other, kn_a)
    y3 = other[0]
    far4 = rows[1] + other[1]
    y4 = flip(far4, "seq", 12)
    y3s = [y3] + [flip(y3, "seq", m) for m in (1, 2, 3)]
    kn_b, vn_b = key_value_part(tie(reach, far4), half, half, "key_value_b")
    y4 = tie(y4, kn_b)
    y4s = [y4] + [flip(y4, "seq", m) for m in (1, 2, 3)]
    arrived = (y1, y2a, y2b, *y3s, *y4s)

    query_grad, total = pl.pallas_call(
        reads_kernel,
        in_specs=[scalar] + [whole] * 17,
        out_specs=[anywhere, whole],
        out_shape=[sds((length, heads * DH), bf16), sds((8, names), f32)],
        scratch_shapes=[
            pltpu.VMEM((heads, DH, 4 * DH), bf16),
            pltpu.VMEM((length, heads * DH), bf16),
            pltpu.SemaphoreType.DMA((length // CHUNK,)),
        ],
        compiler_params=limit(30),
        cost_estimate=cost(6),
        name="reads",
    )(reach, queries, out_grad, w_cols, qn, lam0, index_row, *arrived)

    def returns(order, start, count, held):
        kn, vn = (kn_a, vn_a) if start < half else (kn_b, vn_b)
        shape = sds((length, heads * DH), bf16)

        def kernel(*refs):
            returns_kernel(start, *refs)

        return pl.pallas_call(
            kernel,
            in_specs=[scalar] + [whole] * 15 + [anywhere] * len(held),
            out_specs=[anywhere] * 2,
            out_shape=[shape] * 2,
            scratch_shapes=[
                pltpu.VMEM((length, count * DH), bf16),
                pltpu.VMEM((length, count * DH), bf16),
                pltpu.VMEM((heads, DH, DH), bf16),
                pltpu.SemaphoreType.DMA((2,)),
            ],
            input_output_aliases={16: 0, 17: 1} if held else {},
            compiler_params=limit(20),
            cost_estimate=cost(1),
            name="returns",
        )(order, keys, values, kn, vn, *arrived, *held)

    got = [flip(total, "head", 1)]
    held = returns(tie(reach, total), 0, each, ())
    total = total + tie(got[0], *held)
    for stage, (axis, unit) in enumerate((("head", 2), ("seq", 1), ("seq", 4))):
        got = [flip(total, axis, m * unit) for m in (1, 2, 3)]
        held = returns(tie(reach, total), (stage + 1) * each, each, tuple(held))
        one, two, three = lax.optimization_barrier((*got, *held))[:3]
        total = (total + two) + (one + three)
    table_grad = total[: level_table.shape[0]] / (length * span)
    return query_grad, held[0], held[1], table_grad


def solution(mesh):
    return jax.shard_map(
        local,
        mesh=mesh,
        in_specs=(
            P("seq", "head"),
            P("seq", "head"),
            P("seq", "head"),
            P("seq", "head"),
            P(),
            P("seq"),
            P("seq"),
        ),
        out_specs=(P("seq", "head"), P("seq", "head"), P("seq", "head"), P()),
        check_vma=False,
    )
```

```python
import jax
import jax.numpy as jnp
from jax import lax
from jax.experimental import pallas as pl
from jax.experimental.pallas import tpu as pltpu
from jax.sharding import PartitionSpec as P

DH = 128
CHUNK = 256
SCALE = 1.0 / DH
MIB = 2**20

f32 = jnp.float32
bf16 = jnp.bfloat16


def mm(a, b, ca, cb):
    return lax.dot_general(a, b, (((ca,), (cb,)), ((), ())), preferred_element_type=f32)


def place():
    group = lax.axis_index("seq")
    bits = [jnp.bitwise_and(jnp.right_shift(group, l), 1) for l in range(4)]
    return bits, jnp.bitwise_and(group, 3)


def thirds(x):
    one = x.astype(bf16)
    rest = x - one.astype(f32)
    two = rest.astype(bf16)
    return one, two, (rest - two.astype(f32)).astype(bf16)


def one_hot(index_row, size):
    ids = lax.broadcasted_iota(jnp.int32, (size, index_row.shape[1]), 0)
    return jnp.where(ids == index_row, 1.0, 0.0).astype(bf16)


def states_kernel(reach, index_ref, table_ref, q_hbm, k_hbm, v_hbm, g_hbm, w_ref, near1_ref, near2_ref, keep_ref, send_ref, buf, table, sem):
    far_refs = (keep_ref.at[0], keep_ref.at[1], send_ref.at[1], send_ref.at[0])
    sources = (q_hbm, k_hbm, v_hbm, g_hbm)
    wide = buf.shape[-1]
    each = wide // DH
    bits, spot = place()

    def copy(j, a):
        cols = pl.ds(pl.multiple_of((spot ^ j) * wide, wide), wide)
        return pltpu.make_async_copy(sources[a].at[:, cols], buf.at[j, a], sem.at[j, a])

    for j in range(4):
        for a in range(4):
            copy(j, a).start()
    table[...] = jnp.zeros_like(table)
    table[0 : table_ref.shape[0], :] = table_ref[...]
    level = lax.broadcasted_iota(jnp.int32, table.shape, 0)
    picked = one_hot(index_ref[...], table.shape[1])
    pieces = thirds(jnp.where(level <= reach[0], table[...], 0.0))
    w = mm(pieces[0], picked, 1, 0) + mm(pieces[1], picked, 1, 0) + mm(pieces[2], picked, 1, 0)
    w_ref[...] = w
    for j in range(4):
        for a in range(4):
            copy(j, a).wait()
        for i in range(each):
            c = slice(i * DH, (i + 1) * DH)
            head = (spot ^ j) * each + i
            own = mm(buf[j, 2, :, c].T, buf[j, 1, :, c], 1, 0)
            gt = buf[j, 3, :, c].T.astype(f32)
            parts = [(gt * w[l : l + 1, :]).astype(bf16) for l in range(1, 5)]
            grads = mm(jnp.concatenate(parts, 0), buf[j, 0, :, c], 1, 0)
            xs = [jnp.where(bits[l] > 0, grads[l * DH : (l + 1) * DH], own) for l in range(4)]
            near1_ref[head] = xs[0]
            near2_ref[head] = xs[1]
            far_refs[j][0, i] = xs[2]
            far_refs[j][1, i] = xs[3]


def causal_mask(flip_sides):
    rows = lax.broadcasted_iota(jnp.int32, (CHUNK, CHUNK), 0)
    cols = lax.broadcasted_iota(jnp.int32, (CHUNK, CHUNK), 1)
    return rows <= cols if flip_sides else rows >= cols


def query_kernel(after, q_ref, k_ref, v_ref, g_ref, w_ref, out_ref, lam_ref):
    @pl.when(pl.program_id(0) == 0)
    def _():
        lam_ref[...] = jnp.zeros_like(lam_ref)

    causal = causal_mask(False)
    state = jnp.zeros((DH, DH), f32)
    count = q_ref.shape[0] // CHUNK
    for i in range(count):
        at = pl.ds(i * CHUNK, CHUNK)
        k, v, g = k_ref[at, :], v_ref[at, :], g_ref[at, :]
        near = jnp.where(causal, mm(g, v, 1, 1), 0.0).astype(bf16)
        u = mm(near, k, 1, 0)
        if i > 0:
            u = u + mm(g, state.astype(bf16), 1, 0)
        lam_ref[at, :] += q_ref[at, :].astype(f32) * u
        out_ref[at, :] = (SCALE * w_ref[at, 0:1]) * u
        if i < count - 1:
            state = state + mm(v, k, 0, 0)


def key_value_kernel(after, q_ref, k_ref, v_ref, g_ref, w_ref, key_ref, value_ref):
    causal = causal_mask(True)
    state = jnp.zeros((DH, DH), f32)
    count = q_ref.shape[0] // CHUNK
    for i in reversed(range(count)):
        at = pl.ds(i * CHUNK, CHUNK)
        k, v, g = k_ref[at, :], v_ref[at, :], g_ref[at, :]
        q = (q_ref[at, :].astype(f32) * w_ref[at, 0:1]).astype(bf16)
        near_key = jnp.where(causal, mm(v, g, 1, 1), 0.0).astype(bf16)
        near_value = jnp.where(causal, mm(k, q, 1, 1), 0.0).astype(bf16)
        key = mm(near_key, q, 1, 0)
        value = mm(near_value, g, 1, 0)
        if i < count - 1:
            held = state.astype(bf16)
            key = key + mm(v, held, 1, 0)
            value = value + mm(k, held, 1, 1)
        key_ref[at, :] = SCALE * key
        value_ref[at, :] = SCALE * value
        if i > 0:
            state = state + mm(g, q, 0, 0)


def level_states(keep, y1_ref, y2_ref, y34_refs, bits, head, j, i):
    ys = (y1_ref[head], y2_ref[head], y34_refs[j][0, i], y34_refs[j][1, i])
    return [jnp.where(bits[l] == keep, ys[l], 0.0) for l in range(4)]


def reads_kernel(reach, q_ref, g_ref, w_ref, qn_ref, lam0_ref, index_ref, y1_ref, y2_ref, *rest):
    y34_refs, (out_hbm, table_ref, st, out_buf, sem) = rest[:4], rest[4:]
    length = q_ref.shape[0]
    heads = y1_ref.shape[0]
    each = heads // 4
    tile = CHUNK
    bits, spot = place()
    for j in range(4):
        for i in range(each):
            head = (spot ^ j) * each + i
            parts = level_states(1, y1_ref, y2_ref, y34_refs, bits, head, j, i)
            st[head] = jnp.concatenate(parts, 1).astype(bf16)
    lane = lax.broadcasted_iota(jnp.int32, (1, DH), 1)
    table = None
    copies = []
    for t in range(length // tile):
        at = pl.ds(t * tile, tile)
        w = w_ref[at, :]
        wide = [jnp.broadcast_to(SCALE * w[:, l : l + 1], (tile, DH)) for l in range(1, 5)]
        acc = [None] * 4
        for h in range(heads):
            c = slice(h * DH, (h + 1) * DH)
            reads = mm(g_ref[at, c], st[h], 1, 0)
            q = q_ref[at, c].astype(f32)
            total = qn_ref[at, c]
            for l in range(4):
                read = reads[:, l * DH : (l + 1) * DH]
                product = q * read
                acc[l] = product if acc[l] is None else acc[l] + product
                total = total + wide[l] * read
            out_buf[at, c] = total.astype(bf16)
        copies.append(pltpu.make_async_copy(out_buf.at[at, :], out_hbm.at[at, :], sem.at[t]))
        copies[-1].start()
        lam = jnp.zeros((tile, DH), f32)
        for l, x in enumerate([lam0_ref[at, :]] + acc):
            here = (lane == l) & (reach[0] >= l)
            lam = jnp.where(here, jnp.sum(x, 1, keepdims=True), lam)
        lam = (SCALE * lam).T[:8]
        picked = one_hot(index_ref[:, at], table_ref.shape[1])
        for piece in thirds(lam):
            part = mm(piece, picked, 1, 1)
            table = part if table is None else table + part
    table_ref[...] = table
    for copy in copies:
        copy.wait()


def pair_kernel(keep_ref, got_ref, near_ref, near_got_ref, after, own_ref, send_ref, sum_ref):
    own_ref[...] = keep_ref[0] + got_ref[0]
    send_ref[...] = keep_ref[1] + got_ref[1]
    sum_ref[...] = near_ref[...] + near_got_ref[...]


def rows_kernel(own_ref, got_ref, after, near_in, rows_ref, near_out):
    rows_ref[...] = own_ref[...] + got_ref[...]


def cross_kernel(rows_ref, other_ref, after, after_too, out_ref):
    out_ref[...] = rows_ref[1] + other_ref[1]


def pack_kernel(y3_ref, y4_ref, *rest):
    out_ref = rest[-1]
    out_ref[0] = y3_ref[0]
    out_ref[1] = y4_ref[...]


def returns_kernel(start, order, k_ref, v_ref, kn_ref, vn_ref, y1_ref, y2_ref, *rest):
    y34_refs = rest[:4]
    key_hbm, value_hbm, key_buf, value_buf, st, sem = rest[-6:]
    heads = y1_ref.shape[0]
    each = heads // 4
    count = key_buf.shape[1] // DH
    near_start = start % (kn_ref.shape[1] // DH)
    bits, spot = place()
    for j in range(4):
        for i in range(each):
            head = (spot ^ j) * each + i

            @pl.when((head >= start) & (head < start + count))
            def _():
                parts = level_states(0, y1_ref, y2_ref, y34_refs, bits, head, j, i)
                st[head] = (parts[0] + parts[1] + parts[2] + parts[3]).astype(bf16)

    for i in range(count):
        head = start + i
        c = slice(head * DH, (head + 1) * DH)
        n = slice((near_start + i) * DH, (near_start + i + 1) * DH)
        o = slice(i * DH, (i + 1) * DH)
        key_buf[:, o] = (kn_ref[:, n] + SCALE * mm(v_ref[:, c], st[head], 1, 0)).astype(bf16)
        value_buf[:, o] = (vn_ref[:, n] + SCALE * mm(k_ref[:, c], st[head], 1, 1)).astype(bf16)
    cols = pl.ds(start * DH, count * DH)
    key_copy = pltpu.make_async_copy(key_buf, key_hbm.at[:, cols], sem.at[0])
    value_copy = pltpu.make_async_copy(value_buf, value_hbm.at[:, cols], sem.at[1])
    key_copy.start()
    value_copy.start()
    key_copy.wait()
    value_copy.wait()


def flip(x, axis, mask):
    return lax.ppermute(x, axis, [(i, i ^ mask) for i in range(lax.axis_size(axis))])


def in_hbm(x):
    return pltpu.with_memory_space_constraint(x, pltpu.HBM)


def tie(x, *deps):
    return lax.optimization_barrier((x, *deps))[0]


def local(queries, keys, values, out_grad, level_table, table_index, reach):
    length = queries.shape[0]
    heads = queries.shape[1] // DH
    each = heads // 4
    span = lax.axis_size("seq")
    names = level_table.shape[1]
    index_row = table_index.reshape(1, length)
    sds = jax.ShapeDtypeStruct
    whole = pl.BlockSpec(memory_space=pltpu.VMEM)
    scalar = pl.BlockSpec(memory_space=pltpu.SMEM)
    anywhere = pl.BlockSpec(memory_space=pl.ANY)
    limit = lambda mib: pltpu.CompilerParams(vmem_limit_bytes=mib * MIB)
    cost = pl.CostEstimate(flops=10**8, bytes_accessed=MIB, transcendentals=0)

    w_rows, near, near2, keep, send = pl.pallas_call(
        states_kernel,
        in_specs=[scalar, whole, whole] + [anywhere] * 4,
        out_specs=[whole] * 5,
        out_shape=[sds((8, length), f32)]
        + [sds((heads, DH, DH), f32)] * 2
        + [sds((2, 2, each, DH, DH), f32)] * 2,
        scratch_shapes=[
            pltpu.VMEM((4, 4, length, each * DH), bf16),
            pltpu.VMEM((8, names), f32),
            pltpu.SemaphoreType.DMA((4, 4)),
        ],
        compiler_params=limit(20),
        name="states",
    )(reach, index_row, level_table, *[in_hbm(x) for x in (queries, keys, values, out_grad)])
    w_cols = w_rows.T

    token_spec = lambda start: pl.BlockSpec((length, DH), lambda h: (0, h + start))
    fixed = lambda shape: pl.BlockSpec(shape, lambda h: (0,) * len(shape))

    near_params = pltpu.CompilerParams(
        dimension_semantics=("arbitrary",), vmem_limit_bytes=12 * MIB
    )
    tokens = [in_hbm(x) for x in (queries, keys, values, out_grad)]

    def key_value_part(order, start):
        return pl.pallas_call(
            key_value_kernel,
            grid=(each,),
            in_specs=[anywhere] + [token_spec(start)] * 4 + [fixed((length, 8))],
            out_specs=[token_spec(0)] * 2,
            out_shape=[sds((length, each * DH), f32)] * 2,
            compiler_params=near_params,
            cost_estimate=cost,
            name="key_value",
        )(order, *tokens, w_cols)

    def local_step(kernel, ins, afters, outs, name, aliases=None):
        return pl.pallas_call(
            kernel,
            in_specs=[whole] * len(ins) + [anywhere] * len(afters),
            out_specs=[whole] * (len(outs) - len(aliases or {})) + [anywhere] * len(aliases or {}),
            out_shape=[sds(x, f32) for x in outs],
            input_output_aliases=aliases or {},
            compiler_params=limit(6),
            cost_estimate=cost,
            name=name,
        )(*ins, *afters)

    quarter = keep.shape[1:]
    got, near_got = flip(send, "seq", 3), flip(near2, "seq", 1)
    near_parts = [key_value_part(keep, 0)]
    near_parts.append(key_value_part(near_parts[0][0], each))
    own, send, near_sum = local_step(
        pair_kernel,
        [keep, got, near2, near_got],
        [near_parts[1][0]],
        [quarter, quarter, near2.shape],
        "pair",
    )
    got, y2 = flip(send, "seq", 1), flip(near_sum, "seq", 3)
    near_parts.append(key_value_part(own, 2 * each))
    rows, near = local_step(
        rows_kernel, [own, got], [near_parts[2][0], near], [quarter, near.shape], "rows", {3: 1}
    )
    other, y1 = flip(rows, "seq", 4), flip(near, "seq", 1)
    near_parts.append(key_value_part(rows, 3 * each))
    (far4,) = local_step(
        cross_kernel, [rows, other], [y2, near_parts[3][0]], [quarter[1:]], "cross"
    )
    y4 = flip(far4, "seq", 12)
    (y34,) = local_step(pack_kernel, [other, y4], [y1], [quarter], "pack")
    y34s = [y34] + [flip(y34, "seq", m) for m in (1, 2, 3)]
    qn, lam0 = pl.pallas_call(
        query_kernel,
        grid=(heads,),
        in_specs=[anywhere] + [token_spec(0)] * 4 + [fixed((length, 8))],
        out_specs=[token_spec(0), fixed((length, DH))],
        out_shape=[sds((length, heads * DH), f32), sds((length, DH), f32)],
        compiler_params=near_params,
        cost_estimate=cost,
        name="query",
    )(y34, *tokens, w_cols)

    query_grad, total = pl.pallas_call(
        reads_kernel,
        in_specs=[scalar] + [whole] * 12,
        out_specs=[anywhere, whole],
        out_shape=[sds((length, heads * DH), bf16), sds((8, names), f32)],
        scratch_shapes=[
            pltpu.VMEM((heads, DH, 4 * DH), bf16),
            pltpu.VMEM((length, heads * DH), bf16),
            pltpu.SemaphoreType.DMA((length // CHUNK,)),
        ],
        compiler_params=limit(24),
        cost_estimate=cost,
        name="reads",
    )(reach, queries, out_grad, w_cols, qn, lam0, index_row, y1, y2, *y34s)
    arrived = (y1, y2, *y34s)

    def returns(order, start, count, held):
        kn, vn = near_parts[start // each]
        shape = sds((length, heads * DH), bf16)

        def kernel(*refs):
            returns_kernel(start, *refs)

        return pl.pallas_call(
            kernel,
            in_specs=[scalar] + [whole] * 10 + [anywhere] * len(held),
            out_specs=[anywhere] * 2,
            out_shape=[shape] * 2,
            scratch_shapes=[
                pltpu.VMEM((length, count * DH), bf16),
                pltpu.VMEM((length, count * DH), bf16),
                pltpu.VMEM((heads, DH, DH), bf16),
                pltpu.SemaphoreType.DMA((2,)),
            ],
            input_output_aliases={11: 0, 12: 1} if held else {},
            compiler_params=limit(20),
            cost_estimate=cost,
            name="returns",
        )(order, keys, values, kn, vn, *arrived, *held)

    got = [flip(total, "head", 1)]
    held = returns(tie(reach, total), 0, each, ())
    total = total + tie(got[0], *held)
    for stage, (axis, unit) in enumerate((("head", 2), ("seq", 1), ("seq", 4))):
        got = [flip(total, axis, m * unit) for m in (1, 2, 3)]
        held = returns(tie(reach, total), (stage + 1) * each, each, tuple(held))
        one, two, three = lax.optimization_barrier((*got, *held))[:3]
        total = (total + two) + (one + three)
    table_grad = total[: level_table.shape[0]] / (length * span)
    return query_grad, held[0], held[1], table_grad


def solution(mesh):
    return jax.shard_map(
        local,
        mesh=mesh,
        in_specs=(
            P("seq", "head"),
            P("seq", "head"),
            P("seq", "head"),
            P("seq", "head"),
            P(),
            P("seq"),
            P("seq"),
        ),
        out_specs=(P("seq", "head"), P("seq", "head"), P("seq", "head"), P()),
        check_vma=False,
    )
```

```python
import jax
import jax.numpy as jnp
from jax import lax
from jax.experimental import pallas as pl
from jax.experimental.pallas import tpu as pltpu
from jax.sharding import PartitionSpec as P

DH = 128
CHUNK = 256
SCALE = 1.0 / DH
MIB = 2**20

f32 = jnp.float32
bf16 = jnp.bfloat16


def mm(a, b, ca, cb):
    return lax.dot_general(a, b, (((ca,), (cb,)), ((), ())), preferred_element_type=f32)


def place():
    group = lax.axis_index("seq")
    bits = [jnp.bitwise_and(jnp.right_shift(group, l), 1) for l in range(4)]
    return bits, jnp.bitwise_and(group, 3)


def thirds(x):
    one = x.astype(bf16)
    rest = x - one.astype(f32)
    two = rest.astype(bf16)
    return one, two, (rest - two.astype(f32)).astype(bf16)


def one_hot(index_row, size):
    ids = lax.broadcasted_iota(jnp.int32, (size, index_row.shape[1]), 0)
    return jnp.where(ids == index_row, 1.0, 0.0).astype(bf16)


def states_kernel(
    reach, index_ref, table_ref, q_hbm, k_hbm, v_hbm, g_hbm,
    w_ref, near1_ref, near2_ref, keep_ref, send_ref,
    buf, table, sem,
):
    far_refs = (keep_ref.at[0], keep_ref.at[1], send_ref.at[1], send_ref.at[0])
    sources = (q_hbm, k_hbm, v_hbm, g_hbm)
    wide = buf.shape[-1]
    each = wide // DH
    bits, spot = place()

    def copy(j, a):
        cols = pl.ds(pl.multiple_of((spot ^ j) * wide, wide), wide)
        return pltpu.make_async_copy(sources[a].at[:, cols], buf.at[j, a], sem.at[j, a])

    for j in range(4):
        for a in range(4):
            copy(j, a).start()
    table[...] = jnp.zeros_like(table)
    table[0 : table_ref.shape[0], :] = table_ref[...]
    level = lax.broadcasted_iota(jnp.int32, table.shape, 0)
    picked = one_hot(index_ref[...], table.shape[1])
    pieces = thirds(jnp.where(level <= reach[0], table[...], 0.0))
    w = mm(pieces[0], picked, 1, 0) + mm(pieces[1], picked, 1, 0) + mm(pieces[2], picked, 1, 0)
    w_ref[...] = w
    for j in range(4):
        for a in range(4):
            copy(j, a).wait()
        for i in range(each):
            c = slice(i * DH, (i + 1) * DH)
            head = (spot ^ j) * each + i
            own = mm(buf[j, 2, :, c].T, buf[j, 1, :, c], 1, 0)
            gt = buf[j, 3, :, c].T.astype(f32)
            parts = [(gt * w[l : l + 1, :]).astype(bf16) for l in range(1, 5)]
            grads = mm(jnp.concatenate(parts, 0), buf[j, 0, :, c], 1, 0)
            xs = [jnp.where(bits[l] > 0, grads[l * DH : (l + 1) * DH], own) for l in range(4)]
            near1_ref[head] = xs[0]
            near2_ref[head] = xs[1]
            far_refs[j][0, i] = xs[2]
            far_refs[j][1, i] = xs[3]


def group_kernel(after, q_ref, k_ref, v_ref, g_ref, w_ref, qn_ref, kn_ref, vn_ref, lam_ref):
    rows = lax.broadcasted_iota(jnp.int32, (CHUNK, CHUNK), 0)
    cols = lax.broadcasted_iota(jnp.int32, (CHUNK, CHUNK), 1)
    causal = rows >= cols
    count = q_ref.shape[0] // CHUNK

    @pl.when(pl.program_id(0) == 0)
    def _():
        lam_ref[...] = jnp.zeros_like(lam_ref)

    state = jnp.zeros((DH, DH), f32)
    held = []
    for i in range(count):
        at = pl.ds(i * CHUNK, CHUNK)
        k, v, g = k_ref[at, :], v_ref[at, :], g_ref[at, :]
        q = q_ref[at, :].astype(f32)
        weight = w_ref[at, 0:1]
        scaled = (q * weight).astype(bf16)
        grad_probs = jnp.where(causal, mm(g, v, 1, 1), 0.0).astype(bf16)
        scores = jnp.where(causal, mm(scaled, k, 1, 1), 0.0).astype(bf16)
        u = mm(grad_probs, k, 1, 0)
        if i > 0:
            u = u + mm(g, state.astype(bf16), 1, 0)
        lam_ref[at, :] += q * u
        qn_ref[at, :] = (SCALE * weight) * u
        if i < count - 1:
            state = state + mm(v, k, 0, 0)
        held.append((scaled, grad_probs, scores))
    state = jnp.zeros((DH, DH), f32)
    for i in reversed(range(count)):
        at = pl.ds(i * CHUNK, CHUNK)
        k, v, g = k_ref[at, :], v_ref[at, :], g_ref[at, :]
        scaled, grad_probs, scores = held[i]
        key = mm(grad_probs, scaled, 0, 0)
        value = mm(scores, g, 0, 0)
        if i < count - 1:
            rounded = state.astype(bf16)
            key = key + mm(v, rounded, 1, 0)
            value = value + mm(k, rounded, 1, 1)
        kn_ref[at, :] = SCALE * key
        vn_ref[at, :] = SCALE * value
        if i > 0:
            state = state + mm(g, scaled, 0, 0)


def level_states(keep, y1_ref, y2_ref, y34_refs, bits, head, j, i):
    ys = (y1_ref[head], y2_ref[head], y34_refs[j][0, i], y34_refs[j][1, i])
    return [jnp.where(bits[l] == keep, ys[l], 0.0) for l in range(4)]


def reads_tile(at, levels, q_ref, g_ref, w_ref, st, old, new_ref):
    tile = at.size
    w = w_ref[at, :]
    wide = [jnp.broadcast_to(SCALE * w[:, l : l + 1], (tile, DH)) for l in levels]
    acc = [None] * len(levels)
    for h in range(st.shape[0]):
        c = slice(h * DH, (h + 1) * DH)
        reads = mm(g_ref[at, c], st[h], 1, 0)
        q = q_ref[at, c].astype(f32)
        total = old(h)
        for i in range(len(levels)):
            read = reads[:, i * DH : (i + 1) * DH]
            product = q * read
            acc[i] = product if acc[i] is None else acc[i] + product
            total = total + wide[i] * read
        new_ref[at, c] = total.astype(new_ref.dtype)
    return acc


def near_reads_kernel(after, reach, q_ref, g_ref, w_ref, y1_ref, y2_ref, *rest):
    count = (len(rest) - 3) // 2
    qn_refs, lam_refs, (out_ref, lam_ref, st) = rest[:count], rest[count : 2 * count], rest[2 * count :]
    heads = y1_ref.shape[0]
    each = heads // count
    bits, spot = place()
    for h in range(heads):
        parts = [jnp.where(b > 0, y_ref[h], 0.0) for b, y_ref in zip(bits, (y1_ref, y2_ref))]
        st[h] = jnp.concatenate(parts, 1).astype(bf16)
    lane = lax.broadcasted_iota(jnp.int32, (1, DH), 1)
    for t in range(q_ref.shape[0] // CHUNK):
        at = pl.ds(t * CHUNK, CHUNK)

        def old(h):
            i = h % each
            return qn_refs[h // each][at, i * DH : (i + 1) * DH]

        acc = reads_tile(at, (1, 2), q_ref, g_ref, w_ref, st, old, out_ref)
        lam0 = lam_refs[0][at, :]
        for ref in lam_refs[1:]:
            lam0 = lam0 + ref[at, :]
        lam = jnp.zeros((CHUNK, DH), f32)
        for l, x in enumerate([lam0] + acc):
            here = (lane == l) & (reach[0] >= l)
            lam = jnp.where(here, jnp.sum(x, 1, keepdims=True), lam)
        lam_ref[at, :] = lam


def reads_kernel(reach, q_ref, g_ref, w_ref, qn_ref, lam_ref, index_ref, *rest):
    y34_refs, (out_hbm, table_ref, st, out_buf, sem) = rest[:4], rest[4:]
    heads = st.shape[0]
    each = heads // 4
    bits, spot = place()
    for j in range(4):
        for i in range(each):
            head = (spot ^ j) * each + i
            parts = [jnp.where(bits[l + 2] > 0, y34_refs[j][l, i], 0.0) for l in range(2)]
            st[head] = jnp.concatenate(parts, 1).astype(bf16)
    lane = lax.broadcasted_iota(jnp.int32, (1, DH), 1)
    table = None
    copies = []
    for t in range(q_ref.shape[0] // CHUNK):
        at = pl.ds(t * CHUNK, CHUNK)

        def old(h):
            return qn_ref[at, h * DH : (h + 1) * DH]

        acc = reads_tile(at, (3, 4), q_ref, g_ref, w_ref, st, old, out_buf)
        copies.append(pltpu.make_async_copy(out_buf.at[at, :], out_hbm.at[at, :], sem.at[t]))
        copies[-1].start()
        lam = lam_ref[at, :]
        for l, x in zip((3, 4), acc):
            here = (lane == l) & (reach[0] >= l)
            lam = jnp.where(here, jnp.sum(x, 1, keepdims=True), lam)
        lam = (SCALE * lam).T[:8]
        picked = one_hot(index_ref[:, at], table_ref.shape[1])
        for piece in thirds(lam):
            part = mm(piece, picked, 1, 1)
            table = part if table is None else table + part
    table_ref[...] = table
    for copy in copies:
        copy.wait()


def pair_kernel(keep_ref, got_ref, near_ref, near_got_ref, after, own_ref, send_ref, sum_ref):
    own_ref[...] = keep_ref[0] + got_ref[0]
    send_ref[...] = keep_ref[1] + got_ref[1]
    sum_ref[...] = near_ref[...] + near_got_ref[...]


def rows_kernel(own_ref, got_ref, after, near_in, rows_ref, near_out):
    rows_ref[...] = own_ref[...] + got_ref[...]


def cross_kernel(rows_ref, other_ref, after, after_too, out_ref):
    out_ref[...] = rows_ref[1] + other_ref[1]


def pack_kernel(y3_ref, y4_ref, *rest):
    out_ref = rest[-1]
    out_ref[0] = y3_ref[0]
    out_ref[1] = y4_ref[...]


def returns_kernel(start, order, k_ref, v_ref, kn_ref, vn_ref, y1_ref, y2_ref, *rest):
    y34_refs = rest[:4]
    key_hbm, value_hbm, key_buf, value_buf, st, sem = rest[-6:]
    heads = y1_ref.shape[0]
    each = heads // 4
    count = key_buf.shape[1] // DH
    near_start = start % (kn_ref.shape[1] // DH)
    bits, spot = place()
    for j in range(4):
        for i in range(each):
            head = (spot ^ j) * each + i

            @pl.when((head >= start) & (head < start + count))
            def _():
                parts = level_states(0, y1_ref, y2_ref, y34_refs, bits, head, j, i)
                st[head] = (parts[0] + parts[1] + parts[2] + parts[3]).astype(bf16)

    for i in range(count):
        head = start + i
        c = slice(head * DH, (head + 1) * DH)
        n = slice((near_start + i) * DH, (near_start + i + 1) * DH)
        o = slice(i * DH, (i + 1) * DH)
        key_buf[:, o] = (kn_ref[:, n] + SCALE * mm(v_ref[:, c], st[head], 1, 0)).astype(bf16)
        value_buf[:, o] = (vn_ref[:, n] + SCALE * mm(k_ref[:, c], st[head], 1, 1)).astype(bf16)
    cols = pl.ds(start * DH, count * DH)
    key_copy = pltpu.make_async_copy(key_buf, key_hbm.at[:, cols], sem.at[0])
    value_copy = pltpu.make_async_copy(value_buf, value_hbm.at[:, cols], sem.at[1])
    key_copy.start()
    value_copy.start()
    key_copy.wait()
    value_copy.wait()


def flip(x, axis, mask):
    return lax.ppermute(x, axis, [(i, i ^ mask) for i in range(lax.axis_size(axis))])


def in_hbm(x):
    return pltpu.with_memory_space_constraint(x, pltpu.HBM)


def tie(x, *deps):
    return lax.optimization_barrier((x, *deps))[0]


def local(queries, keys, values, out_grad, level_table, table_index, reach):
    length = queries.shape[0]
    heads = queries.shape[1] // DH
    each = heads // 4
    span = lax.axis_size("seq")
    names = level_table.shape[1]
    index_row = table_index.reshape(1, length)
    sds = jax.ShapeDtypeStruct
    whole = pl.BlockSpec(memory_space=pltpu.VMEM)
    scalar = pl.BlockSpec(memory_space=pltpu.SMEM)
    anywhere = pl.BlockSpec(memory_space=pl.ANY)
    limit = lambda mib: pltpu.CompilerParams(vmem_limit_bytes=mib * MIB)
    cost = pl.CostEstimate(flops=10**8, bytes_accessed=MIB, transcendentals=0)

    w_rows, near, near2, keep, send = pl.pallas_call(
        states_kernel,
        in_specs=[scalar, whole, whole] + [anywhere] * 4,
        out_specs=[whole] * 5,
        out_shape=[sds((8, length), f32)]
        + [sds((heads, DH, DH), f32)] * 2
        + [sds((2, 2, each, DH, DH), f32)] * 2,
        scratch_shapes=[
            pltpu.VMEM((4, 4, length, each * DH), bf16),
            pltpu.VMEM((8, names), f32),
            pltpu.SemaphoreType.DMA((4, 4)),
        ],
        compiler_params=limit(20),
        name="states",
    )(reach, index_row, level_table, *[in_hbm(x) for x in (queries, keys, values, out_grad)])
    w_cols = w_rows.T

    token_spec = lambda start: pl.BlockSpec((length, DH), lambda h: (0, h + start))
    fixed = lambda shape: pl.BlockSpec(shape, lambda h: (0,) * len(shape))

    near_params = pltpu.CompilerParams(
        dimension_semantics=("arbitrary",), vmem_limit_bytes=12 * MIB
    )
    tokens = [in_hbm(x) for x in (queries, keys, values, out_grad)]

    def near_part(after, start):
        return pl.pallas_call(
            group_kernel,
            grid=(each,),
            in_specs=[anywhere] + [token_spec(start)] * 4 + [fixed((length, 8))],
            out_specs=[token_spec(0)] * 3 + [fixed((length, DH))],
            out_shape=[sds((length, each * DH), f32)] * 3 + [sds((length, DH), f32)],
            compiler_params=near_params,
            cost_estimate=cost,
            name="group",
        )(after, *tokens, w_cols)

    def local_step(kernel, ins, afters, outs, name, aliases=None):
        return pl.pallas_call(
            kernel,
            in_specs=[whole] * len(ins) + [anywhere] * len(afters),
            out_specs=[whole] * (len(outs) - len(aliases or {})) + [anywhere] * len(aliases or {}),
            out_shape=[sds(x, f32) for x in outs],
            input_output_aliases=aliases or {},
            compiler_params=limit(6),
            cost_estimate=cost,
            name=name,
        )(*ins, *afters)

    quarter = keep.shape[1:]
    got, near_got = flip(send, "seq", 3), flip(near2, "seq", 1)
    near_parts = [near_part(keep, 0)]
    near_parts.append(near_part(near_parts[0][0], each))
    own, send, near_sum = local_step(
        pair_kernel,
        [keep, got, near2, near_got],
        [near_parts[1][0]],
        [quarter, quarter, near2.shape],
        "pair",
    )
    got, y2 = flip(send, "seq", 1), flip(near_sum, "seq", 3)
    near_parts.append(near_part(own, 2 * each))
    rows, near = local_step(
        rows_kernel, [own, got], [near_parts[2][0], near], [quarter, near.shape], "rows", {3: 1}
    )
    other, y1 = flip(rows, "seq", 4), flip(near, "seq", 1)
    near_parts.append(near_part(rows, 3 * each))
    (far4,) = local_step(
        cross_kernel, [rows, other], [y2, near_parts[3][0]], [quarter[1:]], "cross"
    )
    y4 = flip(far4, "seq", 12)
    (y34,) = local_step(pack_kernel, [other, y4], [y1], [quarter], "pack")
    y34s = [y34] + [flip(y34, "seq", m) for m in (1, 2, 3)]
    qn, lam = pl.pallas_call(
        near_reads_kernel,
        in_specs=[anywhere, scalar] + [whole] * (5 + 2 * len(near_parts)),
        out_specs=[whole] * 2,
        out_shape=[sds((length, heads * DH), f32), sds((length, DH), f32)],
        scratch_shapes=[pltpu.VMEM((heads, DH, 2 * DH), bf16)],
        compiler_params=limit(16),
        cost_estimate=cost,
        name="near_reads",
    )(
        y34, reach, queries, out_grad, w_cols, y1, y2,
        *[p[0] for p in near_parts], *[p[3] for p in near_parts],
    )

    query_grad, total = pl.pallas_call(
        reads_kernel,
        in_specs=[scalar] + [whole] * 10,
        out_specs=[anywhere, whole],
        out_shape=[sds((length, heads * DH), bf16), sds((8, names), f32)],
        scratch_shapes=[
            pltpu.VMEM((heads, DH, 2 * DH), bf16),
            pltpu.VMEM((length, heads * DH), bf16),
            pltpu.SemaphoreType.DMA((length // CHUNK,)),
        ],
        compiler_params=limit(24),
        cost_estimate=cost,
        name="reads",
    )(reach, queries, out_grad, w_cols, qn, lam, index_row, *y34s)
    arrived = (y1, y2, *y34s)

    def returns(order, start, count, held):
        kn, vn = near_parts[start // each][1:3]
        shape = sds((length, heads * DH), bf16)

        def kernel(*refs):
            returns_kernel(start, *refs)

        return pl.pallas_call(
            kernel,
            in_specs=[scalar] + [whole] * 10 + [anywhere] * len(held),
            out_specs=[anywhere] * 2,
            out_shape=[shape] * 2,
            scratch_shapes=[
                pltpu.VMEM((length, count * DH), bf16),
                pltpu.VMEM((length, count * DH), bf16),
                pltpu.VMEM((heads, DH, DH), bf16),
                pltpu.SemaphoreType.DMA((2,)),
            ],
            input_output_aliases={11: 0, 12: 1} if held else {},
            compiler_params=limit(20),
            cost_estimate=cost,
            name="returns",
        )(order, keys, values, kn, vn, *arrived, *held)

    got = [flip(total, "head", 1)]
    held = returns(tie(reach, total), 0, each, ())
    total = total + tie(got[0], *held)
    for stage, (axis, unit) in enumerate((("head", 2), ("seq", 1), ("seq", 4))):
        got = [flip(total, axis, m * unit) for m in (1, 2, 3)]
        held = returns(tie(reach, total), (stage + 1) * each, each, tuple(held))
        one, two, three = lax.optimization_barrier((*got, *held))[:3]
        total = (total + two) + (one + three)
    table_grad = total[: level_table.shape[0]] / (length * span)
    return query_grad, held[0], held[1], table_grad


def solution(mesh):
    return jax.shard_map(
        local,
        mesh=mesh,
        in_specs=(
            P("seq", "head"),
            P("seq", "head"),
            P("seq", "head"),
            P("seq", "head"),
            P(),
            P("seq"),
            P("seq"),
        ),
        out_specs=(P("seq", "head"), P("seq", "head"), P("seq", "head"), P()),
        check_vma=False,
    )
```

```python
import jax
import jax.numpy as jnp
from jax import lax
from jax.experimental import pallas as pl
from jax.experimental.pallas import tpu as pltpu
from jax.sharding import PartitionSpec as P

DH = 128
CHUNK = 256
SCALE = 1.0 / DH
MIB = 2**20

f32 = jnp.float32
bf16 = jnp.bfloat16


def mm(a, b, ca, cb):
    return lax.dot_general(a, b, (((ca,), (cb,)), ((), ())), preferred_element_type=f32)


def place():
    group = lax.axis_index("seq")
    bits = [jnp.bitwise_and(jnp.right_shift(group, l), 1) for l in range(4)]
    return bits, jnp.bitwise_and(group, 3)


def thirds(x):
    one = x.astype(bf16)
    rest = x - one.astype(f32)
    two = rest.astype(bf16)
    return one, two, (rest - two.astype(f32)).astype(bf16)


def one_hot(index_row, size):
    ids = lax.broadcasted_iota(jnp.int32, (size, index_row.shape[1]), 0)
    return jnp.where(ids == index_row, 1.0, 0.0).astype(bf16)


def states_kernel(
    reach, index_ref, table_ref, q_hbm, k_hbm, v_hbm, g_hbm,
    w_ref, near1_ref, near2_ref, keep_ref, send_ref,
    buf, table, sem,
):
    far_refs = (keep_ref.at[0], keep_ref.at[1], send_ref.at[1], send_ref.at[0])
    sources = (q_hbm, k_hbm, v_hbm, g_hbm)
    wide = buf.shape[-1]
    each = wide // DH
    bits, spot = place()

    def copy(j, a):
        cols = pl.ds(pl.multiple_of((spot ^ j) * wide, wide), wide)
        return pltpu.make_async_copy(sources[a].at[:, cols], buf.at[j, a], sem.at[j, a])

    for j in range(4):
        for a in range(4):
            copy(j, a).start()
    table[...] = jnp.zeros_like(table)
    table[0 : table_ref.shape[0], :] = table_ref[...]
    level = lax.broadcasted_iota(jnp.int32, table.shape, 0)
    picked = one_hot(index_ref[...], table.shape[1])
    pieces = thirds(jnp.where(level <= reach[0], table[...], 0.0))
    w = mm(pieces[0], picked, 1, 0) + mm(pieces[1], picked, 1, 0) + mm(pieces[2], picked, 1, 0)
    w_ref[...] = w
    for j in range(4):
        for a in range(4):
            copy(j, a).wait()
        for i in range(each):
            c = slice(i * DH, (i + 1) * DH)
            head = (spot ^ j) * each + i
            own = mm(buf[j, 2, :, c].T, buf[j, 1, :, c], 1, 0)
            gt = buf[j, 3, :, c].T.astype(f32)
            parts = [(gt * w[l : l + 1, :]).astype(bf16) for l in range(1, 5)]
            grads = mm(jnp.concatenate(parts, 0), buf[j, 0, :, c], 1, 0)
            xs = [jnp.where(bits[l] > 0, grads[l * DH : (l + 1) * DH], own) for l in range(4)]
            near1_ref[head] = xs[0]
            near2_ref[head] = xs[1]
            far_refs[j][0, i] = xs[2]
            far_refs[j][1, i] = xs[3]


def group_kernel(after, q_ref, k_ref, v_ref, g_ref, w_ref, qn_ref, kn_ref, vn_ref, lam_ref):
    rows = lax.broadcasted_iota(jnp.int32, (CHUNK, CHUNK), 0)
    cols = lax.broadcasted_iota(jnp.int32, (CHUNK, CHUNK), 1)
    causal = rows >= cols
    count = q_ref.shape[0] // CHUNK

    @pl.when(pl.program_id(0) == 0)
    def _():
        lam_ref[...] = jnp.zeros_like(lam_ref)

    state = jnp.zeros((DH, DH), f32)
    held = []
    for i in range(count):
        at = pl.ds(i * CHUNK, CHUNK)
        k, v, g = k_ref[at, :], v_ref[at, :], g_ref[at, :]
        q = q_ref[at, :].astype(f32)
        weight = w_ref[at, 0:1]
        scaled = (q * weight).astype(bf16)
        grad_probs = jnp.where(causal, mm(g, v, 1, 1), 0.0).astype(bf16)
        scores = jnp.where(causal, mm(scaled, k, 1, 1), 0.0).astype(bf16)
        u = mm(grad_probs, k, 1, 0)
        if i > 0:
            u = u + mm(g, state.astype(bf16), 1, 0)
        lam_ref[at, :] += q * u
        qn_ref[at, :] = (SCALE * weight) * u
        if i < count - 1:
            state = state + mm(v, k, 0, 0)
        held.append((scaled, grad_probs, scores))
    state = jnp.zeros((DH, DH), f32)
    for i in reversed(range(count)):
        at = pl.ds(i * CHUNK, CHUNK)
        k, v, g = k_ref[at, :], v_ref[at, :], g_ref[at, :]
        scaled, grad_probs, scores = held[i]
        key = mm(grad_probs, scaled, 0, 0)
        value = mm(scores, g, 0, 0)
        if i < count - 1:
            rounded = state.astype(bf16)
            key = key + mm(v, rounded, 1, 0)
            value = value + mm(k, rounded, 1, 1)
        kn_ref[at, :] = SCALE * key
        vn_ref[at, :] = SCALE * value
        if i > 0:
            state = state + mm(g, scaled, 0, 0)


def level_states(keep, y1_ref, y2_ref, y34_refs, bits, head, j, i):
    ys = (y1_ref[head], y2_ref[head], y34_refs[j][0, i], y34_refs[j][1, i])
    return [jnp.where(bits[l] == keep, ys[l], 0.0) for l in range(4)]


def reads_tile(at, levels, heads, q_ref, g_ref, w_ref, held, old, put):
    tile = at.size
    w = w_ref[at, :]
    wide = [jnp.broadcast_to(SCALE * w[:, l : l + 1], (tile, DH)) for l in levels]
    acc = [None] * len(levels)
    for n, head in enumerate(heads):
        c = pl.ds(head * DH if isinstance(head, int) else pl.multiple_of(head * DH, DH), DH)
        reads = mm(g_ref[at, c], held[n], 1, 0)
        q = q_ref[at, c].astype(f32)
        total = old(n, c)
        for i in range(len(levels)):
            read = reads[:, i * DH : (i + 1) * DH]
            product = q * read
            acc[i] = product if acc[i] is None else acc[i] + product
            total = total + wide[i] * read
        put(n, c, total)
    return acc


def put_levels(lam, levels, acc, reach):
    lane = lax.broadcasted_iota(jnp.int32, (1, DH), 1)
    for l, x in zip(levels, acc):
        here = (lane == l) & (reach[0] >= l)
        lam = lam + jnp.where(here, jnp.sum(x, 1, keepdims=True), 0.0)
    return lam


def head_spots(refs):
    return [
        (ref, slice(i * DH, (i + 1) * DH)) for ref in refs for i in range(ref.shape[1] // DH)
    ]


def near_reads_kernel(reach, y34_ref, q_ref, g_ref, w_ref, y1_ref, y2_ref, *rest):
    count = (len(rest) - 4) // 2
    qn_refs, lam_refs = rest[:count], rest[count : 2 * count]
    out_ref, lam_ref, late_ref, st = rest[2 * count :]
    heads = y1_ref.shape[0]
    spots = head_spots(qn_refs)
    bits, spot = place()
    late_ref[...] = y34_ref[...]
    for h in range(heads):
        parts = [jnp.where(b > 0, y_ref[h], 0.0) for b, y_ref in zip(bits, (y1_ref, y2_ref))]
        st[h] = jnp.concatenate(parts, 1).astype(bf16)
    for t in range(q_ref.shape[0] // CHUNK):
        at = pl.ds(t * CHUNK, CHUNK)

        def old(n, c):
            ref, cols = spots[n]
            return ref[at, cols]

        def put(n, c, total):
            out_ref[at, c] = total

        acc = reads_tile(at, (1, 2), range(heads), q_ref, g_ref, w_ref, st, old, put)
        lam0 = lam_refs[0][at, :]
        for ref in lam_refs[1:]:
            lam0 = lam0 + ref[at, :]
        lam_ref[at, :] = put_levels(jnp.zeros((CHUNK, DH), f32), (0, 1, 2), [lam0] + acc, reach)


def far_reads(spots, reach, q_ref, g_ref, w_ref, qn_ref, lam_ref, y34_refs, out_hbm, st, out_buf, sem, finish):
    each = y34_refs[0].shape[1]
    bits, spot = place()
    for n, y34_ref in enumerate(y34_refs):
        for i in range(each):
            parts = [jnp.where(bits[l + 2] > 0, y34_ref[l, i], 0.0) for l in range(2)]
            st[n * each + i] = jnp.concatenate(parts, 1).astype(bf16)
    heads = [(spot ^ j) * each + i for j in spots for i in range(each)]
    copies = []
    for t in range(q_ref.shape[0] // CHUNK):
        at = pl.ds(t * CHUNK, CHUNK)

        def old(n, c):
            return qn_ref[at, c]

        def put(n, c, total):
            out_buf[at, n * DH : (n + 1) * DH] = total.astype(bf16)

        acc = reads_tile(at, (3, 4), heads, q_ref, g_ref, w_ref, st, old, put)
        for n, j in enumerate(spots):
            wide = each * DH
            cols = pl.ds(pl.multiple_of((spot ^ j) * wide, wide), wide)
            copies.append(
                pltpu.make_async_copy(
                    out_buf.at[at, pl.ds(n * wide, wide)], out_hbm.at[at, cols], sem.at[t, n]
                )
            )
            copies[-1].start()
        finish(at, put_levels(lam_ref[at, :], (3, 4), acc, reach))
    for copy in copies:
        copy.wait()


FIRST_SPOTS = (0, 1, 3)


def first_reads_kernel(reach, q_ref, g_ref, w_ref, qn_ref, lam_ref, *rest):
    y34_refs, (out_hbm, lam_out, st, out_buf, sem) = rest[:3], rest[3:]

    def finish(at, lam):
        lam_out[at, :] = lam

    far_reads(FIRST_SPOTS, reach, q_ref, g_ref, w_ref, qn_ref, lam_ref, y34_refs, out_hbm, st, out_buf, sem, finish)


def last_reads_kernel(reach, q_ref, g_ref, w_ref, qn_ref, lam_ref, y34_ref, index_ref, held, out_hbm, table_ref, st, out_buf, sem):
    table_ref[...] = jnp.zeros_like(table_ref)

    def finish(at, lam):
        lam = (SCALE * lam).T[:8]
        picked = one_hot(index_ref[:, at], table_ref.shape[1])
        table_ref[...] += sum(mm(piece, picked, 1, 1) for piece in thirds(lam))

    far_reads((2,), reach, q_ref, g_ref, w_ref, qn_ref, lam_ref, (y34_ref,), out_hbm, st, out_buf, sem, finish)


def pair_kernel(keep_ref, got_ref, near_ref, near_got_ref, after, own_ref, send_ref, sum_ref):
    own_ref[...] = keep_ref[0] + got_ref[0]
    send_ref[...] = keep_ref[1] + got_ref[1]
    sum_ref[...] = near_ref[...] + near_got_ref[...]


def gate_kernel(after, near_in, near_out):
    pass


def rows_kernel(own_ref, got_ref, after, three_ref, four_ref):
    three_ref[...] = own_ref[0] + got_ref[0]
    four_ref[...] = own_ref[1] + got_ref[1]


def cross_kernel(rows_ref, other_ref, after, after_too, out_ref):
    out_ref[...] = rows_ref[...] + other_ref[...]


def pack_kernel(y3_ref, y4_ref, *rest):
    out_ref = rest[-1]
    out_ref[0] = y3_ref[...]
    out_ref[1] = y4_ref[...]


def returns_kernel(start, parts, order, k_ref, v_ref, *rest):
    kn_spots, vn_spots = head_spots(rest[:parts]), head_spots(rest[parts : 2 * parts])
    y1_ref, y2_ref, *y34_refs = rest[2 * parts : 2 * parts + 6]
    key_hbm, value_hbm, key_buf, value_buf, st, sem = rest[-6:]
    heads = y1_ref.shape[0]
    each = heads // 4
    count = key_buf.shape[1] // DH
    bits, spot = place()
    for j in range(4):
        for i in range(each):
            head = (spot ^ j) * each + i

            @pl.when((head >= start) & (head < start + count))
            def _():
                levels = level_states(0, y1_ref, y2_ref, y34_refs, bits, head, j, i)
                st[head] = (levels[0] + levels[1] + levels[2] + levels[3]).astype(bf16)

    for i in range(count):
        head = start + i
        c = slice(head * DH, (head + 1) * DH)
        o = slice(i * DH, (i + 1) * DH)
        (kn_ref, kc), (vn_ref, vc) = kn_spots[i], vn_spots[i]
        key_buf[:, o] = (kn_ref[:, kc] + SCALE * mm(v_ref[:, c], st[head], 1, 0)).astype(bf16)
        value_buf[:, o] = (vn_ref[:, vc] + SCALE * mm(k_ref[:, c], st[head], 1, 1)).astype(bf16)
    cols = pl.ds(start * DH, count * DH)
    key_copy = pltpu.make_async_copy(key_buf, key_hbm.at[:, cols], sem.at[0])
    value_copy = pltpu.make_async_copy(value_buf, value_hbm.at[:, cols], sem.at[1])
    key_copy.start()
    value_copy.start()
    key_copy.wait()
    value_copy.wait()


def flip(x, axis, mask):
    return lax.ppermute(x, axis, [(i, i ^ mask) for i in range(lax.axis_size(axis))])


def in_hbm(x):
    return pltpu.with_memory_space_constraint(x, pltpu.HBM)


def tie(x, *deps):
    return lax.optimization_barrier((x, *deps))[0]


def local(queries, keys, values, out_grad, level_table, table_index, reach):
    length = queries.shape[0]
    heads = queries.shape[1] // DH
    each = heads // 4
    span = lax.axis_size("seq")
    names = level_table.shape[1]
    index_row = table_index.reshape(1, length)
    sds = jax.ShapeDtypeStruct
    whole = pl.BlockSpec(memory_space=pltpu.VMEM)
    scalar = pl.BlockSpec(memory_space=pltpu.SMEM)
    anywhere = pl.BlockSpec(memory_space=pl.ANY)
    limit = lambda mib: pltpu.CompilerParams(vmem_limit_bytes=mib * MIB)
    cost = pl.CostEstimate(flops=10**8, bytes_accessed=MIB, transcendentals=0)

    w_rows, near, near2, keep, send = pl.pallas_call(
        states_kernel,
        in_specs=[scalar, whole, whole] + [anywhere] * 4,
        out_specs=[whole] * 5,
        out_shape=[sds((8, length), f32)]
        + [sds((heads, DH, DH), f32)] * 2
        + [sds((2, 2, each, DH, DH), f32)] * 2,
        scratch_shapes=[
            pltpu.VMEM((4, 4, length, each * DH), bf16),
            pltpu.VMEM((8, names), f32),
            pltpu.SemaphoreType.DMA((4, 4)),
        ],
        compiler_params=limit(20),
        name="states",
    )(reach, index_row, level_table, *[in_hbm(x) for x in (queries, keys, values, out_grad)])
    w_cols = w_rows.T

    token_spec = lambda start: pl.BlockSpec((length, DH), lambda h: (0, h + start))
    fixed = lambda shape: pl.BlockSpec(shape, lambda h: (0,) * len(shape))

    near_params = pltpu.CompilerParams(
        dimension_semantics=("arbitrary",), vmem_limit_bytes=12 * MIB
    )
    tokens = [in_hbm(x) for x in (queries, keys, values, out_grad)]

    def near_part(after, start, count=each):
        return pl.pallas_call(
            group_kernel,
            grid=(count,),
            in_specs=[anywhere] + [token_spec(start)] * 4 + [fixed((length, 8))],
            out_specs=[token_spec(0)] * 3 + [fixed((length, DH))],
            out_shape=[sds((length, count * DH), f32)] * 3 + [sds((length, DH), f32)],
            compiler_params=near_params,
            cost_estimate=cost,
            name="group",
        )(after, *tokens, w_cols)

    def local_step(kernel, ins, afters, outs, name, aliases=None):
        return pl.pallas_call(
            kernel,
            in_specs=[whole] * len(ins) + [anywhere] * len(afters),
            out_specs=[whole] * (len(outs) - len(aliases or {})) + [anywhere] * len(aliases or {}),
            out_shape=[sds(x, f32) for x in outs],
            input_output_aliases=aliases or {},
            compiler_params=limit(6),
            cost_estimate=cost,
            name=name,
        )(*ins, *afters)

    quarter = keep.shape[1:]
    got, near_got = flip(send, "seq", 3), flip(near2, "seq", 1)
    near_parts = [near_part(keep, 0)]
    near_parts.append(near_part(near_parts[0][0], each))
    own, send, near_sum = local_step(
        pair_kernel,
        [keep, got, near2, near_got],
        [near_parts[1][0]],
        [quarter, quarter, near2.shape],
        "pair",
    )
    got, y2 = flip(send, "seq", 1), flip(near_sum, "seq", 3)
    near_parts.append(near_part(own, 2 * each))
    (near,) = local_step(gate_kernel, [], [near_parts[2][0], near], [near.shape], "gate", {1: 0})
    y1 = flip(near, "seq", 1)
    three, four = local_step(
        rows_kernel, [own, got], [near_parts[2][0]], [quarter[1:]] * 2, "rows"
    )
    other4, y3 = flip(four, "seq", 4), flip(three, "seq", 4)
    near_parts.append(near_part(four, 3 * each, each // 2))
    (far4,) = local_step(
        cross_kernel, [four, other4], [y2, near_parts[3][0]], [quarter[1:]], "cross"
    )
    y4 = flip(far4, "seq", 12)
    near_parts.append(near_part(far4, 3 * each + each // 2, each // 2))
    (y34,) = local_step(pack_kernel, [y3, y4], [y1, near_parts[4][0]], [quarter], "pack")
    y34_one, y34_three = flip(y34, "seq", 1), flip(y34, "seq", 3)
    qn, lam, y34_late = pl.pallas_call(
        near_reads_kernel,
        in_specs=[scalar] + [whole] * (6 + 2 * len(near_parts)),
        out_specs=[whole] * 3,
        out_shape=[sds((length, heads * DH), f32), sds((length, DH), f32), sds(quarter, f32)],
        scratch_shapes=[pltpu.VMEM((heads, DH, 2 * DH), bf16)],
        compiler_params=limit(16),
        cost_estimate=cost,
        name="near_reads",
    )(
        reach, y34, queries, out_grad, w_cols, y1, y2,
        *[p[0] for p in near_parts], *[p[3] for p in near_parts],
    )
    y34_two = flip(y34_late, "seq", 2)
    y34s = [y34, y34_one, y34_two, y34_three]

    def far_part(kernel, count, ins, afters, more_out, aliases, name):
        return pl.pallas_call(
            kernel,
            in_specs=[scalar] + [whole] * (5 + len(ins)) + [anywhere] * len(afters),
            out_specs=[anywhere, whole],
            out_shape=[sds((length, heads * DH), bf16), more_out],
            input_output_aliases=aliases,
            scratch_shapes=[
                pltpu.VMEM((count * each, DH, 2 * DH), bf16),
                pltpu.VMEM((length, count * each * DH), bf16),
                pltpu.SemaphoreType.DMA((length // CHUNK, count)),
            ],
            compiler_params=limit(16),
            cost_estimate=cost,
            name=name,
        )(reach, queries, out_grad, w_cols, qn, lam, *ins, *afters)

    query_grad, lam = far_part(
        first_reads_kernel,
        len(FIRST_SPOTS),
        [y34s[j] for j in FIRST_SPOTS],
        [],
        sds((length, DH), f32),
        {},
        "first_reads",
    )
    query_grad, total = far_part(
        last_reads_kernel, 1, [y34_two, index_row], [query_grad], sds((8, names), f32), {8: 0}, "last_reads"
    )
    arrived = (y1, y2, *y34s)

    def returns(order, start, count, held):
        pieces = near_parts[3:] if start == 3 * each else [near_parts[start // each]]
        ins = [keys, values] + [p[1] for p in pieces] + [p[2] for p in pieces] + list(arrived)
        shape = sds((length, heads * DH), bf16)

        def kernel(*refs):
            returns_kernel(start, len(pieces), *refs)

        return pl.pallas_call(
            kernel,
            in_specs=[scalar] + [whole] * len(ins) + [anywhere] * len(held),
            out_specs=[anywhere] * 2,
            out_shape=[shape] * 2,
            scratch_shapes=[
                pltpu.VMEM((length, count * DH), bf16),
                pltpu.VMEM((length, count * DH), bf16),
                pltpu.VMEM((heads, DH, DH), bf16),
                pltpu.SemaphoreType.DMA((2,)),
            ],
            input_output_aliases={len(ins) + 1: 0, len(ins) + 2: 1} if held else {},
            compiler_params=limit(20),
            cost_estimate=cost,
            name="returns",
        )(order, *ins, *held)

    got = [flip(total, "head", 1)]
    held = returns(tie(reach, total), 0, each, ())
    total = total + tie(got[0], *held)
    for stage, (axis, unit) in enumerate((("head", 2), ("seq", 1), ("seq", 4))):
        got = [flip(total, axis, m * unit) for m in (1, 2, 3)]
        held = returns(tie(reach, total), (stage + 1) * each, each, tuple(held))
        one, two, three = lax.optimization_barrier((*got, *held))[:3]
        total = (total + two) + (one + three)
    table_grad = total[: level_table.shape[0]] / (length * span)
    return query_grad, held[0], held[1], table_grad


def solution(mesh):
    return jax.shard_map(
        local,
        mesh=mesh,
        in_specs=(
            P("seq", "head"),
            P("seq", "head"),
            P("seq", "head"),
            P("seq", "head"),
            P(),
            P("seq"),
            P("seq"),
        ),
        out_specs=(P("seq", "head"), P("seq", "head"), P("seq", "head"), P()),
        check_vma=False,
    )
```

```python
import jax
import jax.numpy as jnp
from jax import lax
from jax.experimental import pallas as pl
from jax.experimental.pallas import tpu as pltpu
from jax.sharding import PartitionSpec as P

DH = 128
CHUNK = 256
SCALE = 1.0 / DH
MIB = 2**20

f32 = jnp.float32
bf16 = jnp.bfloat16


def mm(a, b, ca, cb):
    return lax.dot_general(a, b, (((ca,), (cb,)), ((), ())), preferred_element_type=f32)


def place():
    group = lax.axis_index("seq")
    bits = [jnp.bitwise_and(jnp.right_shift(group, l), 1) for l in range(4)]
    return bits, jnp.bitwise_and(group, 3)


def exact_dot(x, y, cx, cy):
    one = x.astype(bf16).astype(f32)
    rest = x - one
    two = rest.astype(bf16).astype(f32)
    stacked = jnp.concatenate([one, two, rest - two, jnp.zeros_like(x)], 0).astype(bf16)
    out = mm(stacked, y, cx, cy)
    return out[0:8] + out[8:16] + out[16:24]


def one_hot(index_row, size):
    ids = lax.broadcasted_iota(jnp.int32, (size, index_row.shape[1]), 0)
    return jnp.where(ids == index_row, 1.0, 0.0).astype(bf16)


def states_kernel(
    reach, index_ref, table_ref, q_hbm, k_hbm, v_hbm, g_hbm,
    w_ref, near1_ref, near2_ref, keep_ref, send_ref,
    buf, table, sem,
):
    far_refs = (keep_ref.at[0], keep_ref.at[1], send_ref.at[1], send_ref.at[0])
    sources = (q_hbm, k_hbm, v_hbm, g_hbm)
    wide = buf.shape[-1]
    each = wide // DH
    bits, spot = place()

    def copy(j, a):
        cols = pl.ds(pl.multiple_of((spot ^ j) * wide, wide), wide)
        return pltpu.make_async_copy(sources[a].at[:, cols], buf.at[j, a], sem.at[j, a])

    for j in range(4):
        for a in range(4):
            copy(j, a).start()
    table[...] = jnp.zeros_like(table)
    table[0 : table_ref.shape[0], :] = table_ref[...]
    level = lax.broadcasted_iota(jnp.int32, table.shape, 0)
    picked = one_hot(index_ref[...], table.shape[1])
    w = exact_dot(jnp.where(level <= reach[0], table[...], 0.0), picked, 1, 0)
    w_ref[...] = w
    for j in range(4):
        for a in range(4):
            copy(j, a).wait()
        for i in range(each):
            c = slice(i * DH, (i + 1) * DH)
            head = (spot ^ j) * each + i
            own = mm(buf[j, 2, :, c].T, buf[j, 1, :, c], 1, 0)
            gt = buf[j, 3, :, c].T.astype(f32)
            parts = [(gt * w[l : l + 1, :]).astype(bf16) for l in range(1, 5)]
            grads = mm(jnp.concatenate(parts, 0), buf[j, 0, :, c], 1, 0)
            xs = [jnp.where(bits[l] > 0, grads[l * DH : (l + 1) * DH], own) for l in range(4)]
            near1_ref[head] = xs[0]
            near2_ref[head] = xs[1]
            far_refs[j][0, i] = xs[2]
            far_refs[j][1, i] = xs[3]


def group_kernel(after, q_ref, k_ref, v_ref, g_ref, w_ref, qn_ref, kn_ref, vn_ref, lam_ref):
    rows = lax.broadcasted_iota(jnp.int32, (CHUNK, CHUNK), 0)
    cols = lax.broadcasted_iota(jnp.int32, (CHUNK, CHUNK), 1)
    causal = rows >= cols
    count = q_ref.shape[0] // CHUNK

    @pl.when(pl.program_id(0) == 0)
    def _():
        lam_ref[...] = jnp.zeros_like(lam_ref)

    state = jnp.zeros((DH, DH), f32)
    held = []
    for i in range(count):
        at = pl.ds(i * CHUNK, CHUNK)
        k, v, g = k_ref[at, :], v_ref[at, :], g_ref[at, :]
        q = q_ref[at, :].astype(f32)
        weight = w_ref[at, 0:1]
        scaled = (q * weight).astype(bf16)
        grad_probs = jnp.where(causal, mm(g, v, 1, 1), 0.0).astype(bf16)
        scores = jnp.where(causal, mm(scaled, k, 1, 1), 0.0).astype(bf16)
        u = mm(grad_probs, k, 1, 0)
        if i > 0:
            u = u + mm(g, state.astype(bf16), 1, 0)
        lam_ref[at, :] += q * u
        qn_ref[at, :] = (SCALE * weight) * u
        if i < count - 1:
            state = state + mm(v, k, 0, 0)
        held.append((scaled, grad_probs, scores))
    state = jnp.zeros((DH, DH), f32)
    for i in reversed(range(count)):
        at = pl.ds(i * CHUNK, CHUNK)
        k, v, g = k_ref[at, :], v_ref[at, :], g_ref[at, :]
        scaled, grad_probs, scores = held[i]
        key = mm(grad_probs, scaled, 0, 0)
        value = mm(scores, g, 0, 0)
        if i < count - 1:
            rounded = state.astype(bf16)
            key = key + mm(v, rounded, 1, 0)
            value = value + mm(k, rounded, 1, 1)
        kn_ref[at, :] = SCALE * key
        vn_ref[at, :] = SCALE * value
        if i > 0:
            state = state + mm(g, scaled, 0, 0)


def level_states(keep, y1_ref, y2_ref, y34_refs, bits, head, j, i):
    ys = (y1_ref[head], y2_ref[head], y34_refs[j][0, i], y34_refs[j][1, i])
    return [jnp.where(bits[l] == keep, ys[l], 0.0) for l in range(4)]


def reads_tile(at, levels, heads, q_ref, g_ref, w_ref, held, old, put):
    tile = at.size
    w = w_ref[at, :]
    wide = [jnp.broadcast_to(SCALE * w[:, l : l + 1], (tile, DH)) for l in levels]
    acc = [None] * len(levels)
    for n, head in enumerate(heads):
        c = pl.ds(head * DH if isinstance(head, int) else pl.multiple_of(head * DH, DH), DH)
        reads = mm(g_ref[at, c], held[n], 1, 0)
        q = q_ref[at, c].astype(f32)
        total = old(n, c)
        for i in range(len(levels)):
            read = reads[:, i * DH : (i + 1) * DH]
            product = q * read
            acc[i] = product if acc[i] is None else acc[i] + product
            total = total + wide[i] * read
        put(n, c, total)
    return acc


def put_levels(lam, levels, acc, reach):
    lane = lax.broadcasted_iota(jnp.int32, (1, DH), 1)
    for l, x in zip(levels, acc):
        here = (lane == l) & (reach[0] >= l)
        lam = lam + jnp.where(here, jnp.sum(x, 1, keepdims=True), 0.0)
    return lam


def head_spots(refs):
    return [
        (ref, slice(i * DH, (i + 1) * DH)) for ref in refs for i in range(ref.shape[1] // DH)
    ]


def near_reads_kernel(reach, y34_ref, q_ref, g_ref, w_ref, y1_ref, y2_ref, *rest):
    count = (len(rest) - 4) // 2
    qn_refs, lam_refs = rest[:count], rest[count : 2 * count]
    out_ref, lam_ref, late_ref, st = rest[2 * count :]
    heads = y1_ref.shape[0]
    spots = head_spots(qn_refs)
    bits, spot = place()
    late_ref[...] = y34_ref[...]
    for h in range(heads):
        parts = [jnp.where(b > 0, y_ref[h], 0.0) for b, y_ref in zip(bits, (y1_ref, y2_ref))]
        st[h] = jnp.concatenate(parts, 1).astype(bf16)
    for t in range(q_ref.shape[0] // CHUNK):
        at = pl.ds(t * CHUNK, CHUNK)

        def old(n, c):
            ref, cols = spots[n]
            return ref[at, cols]

        def put(n, c, total):
            out_ref[at, c] = total

        acc = reads_tile(at, (1, 2), range(heads), q_ref, g_ref, w_ref, st, old, put)
        lam0 = lam_refs[0][at, :]
        for ref in lam_refs[1:]:
            lam0 = lam0 + ref[at, :]
        lam_ref[at, :] = put_levels(jnp.zeros((CHUNK, DH), f32), (0, 1, 2), [lam0] + acc, reach)


def far_reads(spots, reach, q_ref, g_ref, w_ref, qn_ref, lam_ref, y34_refs, out_hbm, st, out_buf, sem, finish):
    each = y34_refs[0].shape[1]
    bits, spot = place()
    for n, y34_ref in enumerate(y34_refs):
        for i in range(each):
            parts = [jnp.where(bits[l + 2] > 0, y34_ref[l, i], 0.0) for l in range(2)]
            st[n * each + i] = jnp.concatenate(parts, 1).astype(bf16)
    heads = [(spot ^ j) * each + i for j in spots for i in range(each)]
    copies = []
    for t in range(q_ref.shape[0] // CHUNK):
        at = pl.ds(t * CHUNK, CHUNK)

        def old(n, c):
            return qn_ref[at, c]

        def put(n, c, total):
            out_buf[at, n * DH : (n + 1) * DH] = total.astype(bf16)

        acc = reads_tile(at, (3, 4), heads, q_ref, g_ref, w_ref, st, old, put)
        for n, j in enumerate(spots):
            wide = each * DH
            cols = pl.ds(pl.multiple_of((spot ^ j) * wide, wide), wide)
            copies.append(
                pltpu.make_async_copy(
                    out_buf.at[at, pl.ds(n * wide, wide)], out_hbm.at[at, cols], sem.at[t, n]
                )
            )
            copies[-1].start()
        finish(at, put_levels(lam_ref[at, :], (3, 4), acc, reach))
    for copy in copies:
        copy.wait()


FIRST_SPOTS = (0, 1, 3)


def first_reads_kernel(reach, q_ref, g_ref, w_ref, qn_ref, lam_ref, *rest):
    y34_refs, index_ref, (out_hbm, lam_out, picked_out, st, out_buf, sem) = rest[:3], rest[3], rest[4:]

    def finish(at, lam):
        lam_out[at, :] = lam
        picked_out[at, :] = one_hot(index_ref[:, at], picked_out.shape[1]).T

    far_reads(FIRST_SPOTS, reach, q_ref, g_ref, w_ref, qn_ref, lam_ref, y34_refs, out_hbm, st, out_buf, sem, finish)


def last_reads_kernel(reach, q_ref, g_ref, w_ref, qn_ref, lam_ref, y34_ref, picked_ref, held, out_hbm, table_ref, st, out_buf, sem):
    table_ref[...] = jnp.zeros_like(table_ref)

    def finish(at, lam):
        lam = (SCALE * lam).T[:8]
        table_ref[...] += exact_dot(lam, picked_ref[at, :], 1, 0)

    far_reads((2,), reach, q_ref, g_ref, w_ref, qn_ref, lam_ref, (y34_ref,), out_hbm, st, out_buf, sem, finish)


def pair_kernel(keep_ref, got_ref, near_ref, near_got_ref, after, own_ref, send_ref, sum_ref):
    own_ref[...] = keep_ref[0] + got_ref[0]
    send_ref[...] = keep_ref[1] + got_ref[1]
    sum_ref[...] = near_ref[...] + near_got_ref[...]


def gate_kernel(after, near_in, near_out):
    pass


def rows_kernel(own_ref, got_ref, after, three_ref, four_ref):
    three_ref[...] = own_ref[0] + got_ref[0]
    four_ref[...] = own_ref[1] + got_ref[1]


def cross_kernel(rows_ref, other_ref, after, after_too, out_ref):
    out_ref[...] = rows_ref[...] + other_ref[...]


def pack_kernel(y3_ref, y4_ref, *rest):
    out_ref = rest[-1]
    out_ref[0] = y3_ref[...]
    out_ref[1] = y4_ref[...]


def returns_kernel(start, parts, order, k_ref, v_ref, *rest):
    kn_spots, vn_spots = head_spots(rest[:parts]), head_spots(rest[parts : 2 * parts])
    y1_ref, y2_ref, *y34_refs = rest[2 * parts : 2 * parts + 6]
    key_hbm, value_hbm, key_buf, value_buf, st, sem = rest[-6:]
    heads = y1_ref.shape[0]
    each = heads // 4
    count = key_buf.shape[1] // DH
    bits, spot = place()
    for j in range(4):
        for i in range(each):
            head = (spot ^ j) * each + i

            @pl.when((head >= start) & (head < start + count))
            def _():
                levels = level_states(0, y1_ref, y2_ref, y34_refs, bits, head, j, i)
                st[head] = (levels[0] + levels[1] + levels[2] + levels[3]).astype(bf16)

    for i in range(count):
        head = start + i
        c = slice(head * DH, (head + 1) * DH)
        o = slice(i * DH, (i + 1) * DH)
        (kn_ref, kc), (vn_ref, vc) = kn_spots[i], vn_spots[i]
        key_buf[:, o] = (kn_ref[:, kc] + SCALE * mm(v_ref[:, c], st[head], 1, 0)).astype(bf16)
        value_buf[:, o] = (vn_ref[:, vc] + SCALE * mm(k_ref[:, c], st[head], 1, 1)).astype(bf16)
    cols = pl.ds(start * DH, count * DH)
    key_copy = pltpu.make_async_copy(key_buf, key_hbm.at[:, cols], sem.at[0])
    value_copy = pltpu.make_async_copy(value_buf, value_hbm.at[:, cols], sem.at[1])
    key_copy.start()
    value_copy.start()
    key_copy.wait()
    value_copy.wait()


def flip(x, axis, mask):
    return lax.ppermute(x, axis, [(i, i ^ mask) for i in range(lax.axis_size(axis))])


def in_hbm(x):
    return pltpu.with_memory_space_constraint(x, pltpu.HBM)


def tie(x, *deps):
    return lax.optimization_barrier((x, *deps))[0]


def local(queries, keys, values, out_grad, level_table, table_index, reach):
    length = queries.shape[0]
    heads = queries.shape[1] // DH
    each = heads // 4
    span = lax.axis_size("seq")
    names = level_table.shape[1]
    index_row = table_index.reshape(1, length)
    sds = jax.ShapeDtypeStruct
    whole = pl.BlockSpec(memory_space=pltpu.VMEM)
    scalar = pl.BlockSpec(memory_space=pltpu.SMEM)
    anywhere = pl.BlockSpec(memory_space=pl.ANY)
    limit = lambda mib: pltpu.CompilerParams(vmem_limit_bytes=mib * MIB)
    cost = pl.CostEstimate(flops=10**8, bytes_accessed=MIB, transcendentals=0)

    w_rows, near, near2, keep, send = pl.pallas_call(
        states_kernel,
        in_specs=[scalar, whole, whole] + [anywhere] * 4,
        out_specs=[whole] * 5,
        out_shape=[sds((8, length), f32)]
        + [sds((heads, DH, DH), f32)] * 2
        + [sds((2, 2, each, DH, DH), f32)] * 2,
        scratch_shapes=[
            pltpu.VMEM((4, 4, length, each * DH), bf16),
            pltpu.VMEM((8, names), f32),
            pltpu.SemaphoreType.DMA((4, 4)),
        ],
        compiler_params=limit(20),
        name="states",
    )(reach, index_row, level_table, *[in_hbm(x) for x in (queries, keys, values, out_grad)])
    w_cols = w_rows.T

    token_spec = lambda start: pl.BlockSpec((length, DH), lambda h: (0, h + start))
    fixed = lambda shape: pl.BlockSpec(shape, lambda h: (0,) * len(shape))

    near_params = pltpu.CompilerParams(
        dimension_semantics=("arbitrary",), vmem_limit_bytes=12 * MIB
    )
    tokens = [in_hbm(x) for x in (queries, keys, values, out_grad)]

    def near_part(after, start, count=each):
        return pl.pallas_call(
            group_kernel,
            grid=(count,),
            in_specs=[anywhere] + [token_spec(start)] * 4 + [fixed((length, 8))],
            out_specs=[token_spec(0)] * 3 + [fixed((length, DH))],
            out_shape=[sds((length, count * DH), f32)] * 3 + [sds((length, DH), f32)],
            compiler_params=near_params,
            cost_estimate=cost,
            name="group",
        )(after, *tokens, w_cols)

    def local_step(kernel, ins, afters, outs, name, aliases=None):
        return pl.pallas_call(
            kernel,
            in_specs=[whole] * len(ins) + [anywhere] * len(afters),
            out_specs=[whole] * (len(outs) - len(aliases or {})) + [anywhere] * len(aliases or {}),
            out_shape=[sds(x, f32) for x in outs],
            input_output_aliases=aliases or {},
            compiler_params=limit(6),
            cost_estimate=cost,
            name=name,
        )(*ins, *afters)

    quarter = keep.shape[1:]
    got, near_got = flip(send, "seq", 3), flip(near2, "seq", 1)
    near_parts = [near_part(keep, 0)]
    near_parts.append(near_part(near_parts[0][0], each))
    own, send, near_sum = local_step(
        pair_kernel,
        [keep, got, near2, near_got],
        [near_parts[1][0]],
        [quarter, quarter, near2.shape],
        "pair",
    )
    got, y2 = flip(send, "seq", 1), flip(near_sum, "seq", 3)
    near_parts.append(near_part(own, 2 * each))
    (near,) = local_step(gate_kernel, [], [near_parts[2][0], near], [near.shape], "gate", {1: 0})
    y1 = flip(near, "seq", 1)
    three, four = local_step(
        rows_kernel, [own, got], [near_parts[2][0]], [quarter[1:]] * 2, "rows"
    )
    other4, y3 = flip(four, "seq", 4), flip(three, "seq", 4)
    near_parts.append(near_part(four, 3 * each, each // 2))
    (far4,) = local_step(
        cross_kernel, [four, other4], [y2, near_parts[3][0]], [quarter[1:]], "cross"
    )
    y4 = flip(far4, "seq", 12)
    near_parts.append(near_part(far4, 3 * each + each // 2, each // 2))
    (y34,) = local_step(pack_kernel, [y3, y4], [y1, near_parts[4][0]], [quarter], "pack")
    y34_one, y34_three = flip(y34, "seq", 1), flip(y34, "seq", 3)
    qn, lam, y34_late = pl.pallas_call(
        near_reads_kernel,
        in_specs=[scalar] + [whole] * (6 + 2 * len(near_parts)),
        out_specs=[whole] * 3,
        out_shape=[sds((length, heads * DH), f32), sds((length, DH), f32), sds(quarter, f32)],
        scratch_shapes=[pltpu.VMEM((heads, DH, 2 * DH), bf16)],
        compiler_params=limit(16),
        cost_estimate=cost,
        name="near_reads",
    )(
        reach, y34, queries, out_grad, w_cols, y1, y2,
        *[p[0] for p in near_parts], *[p[3] for p in near_parts],
    )
    y34_two = flip(y34_late, "seq", 2)
    y34s = [y34, y34_one, y34_two, y34_three]

    def far_part(kernel, count, ins, afters, more_out, aliases, name):
        return pl.pallas_call(
            kernel,
            in_specs=[scalar] + [whole] * (5 + len(ins)) + [anywhere] * len(afters),
            out_specs=[anywhere] + [whole] * len(more_out),
            out_shape=[sds((length, heads * DH), bf16)] + more_out,
            input_output_aliases=aliases,
            scratch_shapes=[
                pltpu.VMEM((count * each, DH, 2 * DH), bf16),
                pltpu.VMEM((length, count * each * DH), bf16),
                pltpu.SemaphoreType.DMA((length // CHUNK, count)),
            ],
            compiler_params=limit(16),
            cost_estimate=cost,
            name=name,
        )(reach, queries, out_grad, w_cols, qn, lam, *ins, *afters)

    query_grad, lam, picked = far_part(
        first_reads_kernel,
        len(FIRST_SPOTS),
        [y34s[j] for j in FIRST_SPOTS] + [index_row],
        [],
        [sds((length, DH), f32), sds((length, names), bf16)],
        {},
        "first_reads",
    )
    query_grad, total = far_part(
        last_reads_kernel, 1, [y34_two, picked], [query_grad], [sds((8, names), f32)], {8: 0}, "last_reads"
    )
    arrived = (y1, y2, *y34s)

    def returns(order, start, count, held):
        pieces = near_parts[3:] if start == 3 * each else [near_parts[start // each]]
        ins = [keys, values] + [p[1] for p in pieces] + [p[2] for p in pieces] + list(arrived)
        shape = sds((length, heads * DH), bf16)

        def kernel(*refs):
            returns_kernel(start, len(pieces), *refs)

        return pl.pallas_call(
            kernel,
            in_specs=[scalar] + [whole] * len(ins) + [anywhere] * len(held),
            out_specs=[anywhere] * 2,
            out_shape=[shape] * 2,
            scratch_shapes=[
                pltpu.VMEM((length, count * DH), bf16),
                pltpu.VMEM((length, count * DH), bf16),
                pltpu.VMEM((heads, DH, DH), bf16),
                pltpu.SemaphoreType.DMA((2,)),
            ],
            input_output_aliases={len(ins) + 1: 0, len(ins) + 2: 1} if held else {},
            compiler_params=limit(20),
            cost_estimate=cost,
            name="returns",
        )(order, *ins, *held)

    got = [flip(total, "head", 1)]
    held = returns(tie(reach, total), 0, each, ())
    total = total + tie(got[0], *held)
    for stage, (axis, unit) in enumerate((("head", 2), ("seq", 1), ("seq", 4))):
        got = [flip(total, axis, m * unit) for m in (1, 2, 3)]
        held = returns(tie(reach, total), (stage + 1) * each, each, tuple(held))
        one, two, three = lax.optimization_barrier((*got, *held))[:3]
        total = (total + two) + (one + three)
    table_grad = total[: level_table.shape[0]] / (length * span)
    return query_grad, held[0], held[1], table_grad


def solution(mesh):
    return jax.shard_map(
        local,
        mesh=mesh,
        in_specs=(
            P("seq", "head"),
            P("seq", "head"),
            P("seq", "head"),
            P("seq", "head"),
            P(),
            P("seq"),
            P("seq"),
        ),
        out_specs=(P("seq", "head"), P("seq", "head"), P("seq", "head"), P()),
        check_vma=False,
    )
```
